256 devices in a mesh: member: 32 (over z_hi, y, core), tile: 8 (over x, z_lo).
Axes of the slice: x: 4, y: 4, z: 8 (z_hi: 4, z_lo: 2; z = z_hi * 2 + z_lo), core: 2. Of those that a mesh axis runs over, the one named last changes fastest.
Arguments:
- ensemble: float32 [64, 512, 4096], P('member', 'tile'), may hold values from -6 to 6
- velocity: float32 [2, 512, 4096], P(None, 'tile'), may hold values from -0.45 to 0.45
- observed_column: int32 [512, 32, 32], P('tile', 'member'), may hold values from 0 to 127
- observation_slot_count: int32 [512, 32], P('tile', 'member'), may hold values from 1 to 32
- local_radius: int32 [512, 32], P('tile', 'member'), may hold values from 16 to 128
- observed_value: float32 [512, 32, 32], P('tile', 'member'), may hold values from -9 to 9
- error_variance: float32 [512, 32, 32], P('tile', 'member'), may hold values from 0.25 to 2
Outputs:
- analysis: float32 [64, 512, 4096], P('member', 'tile')
The draws below stay inside these ranges and needn't reach their ends.
All inputs are finite; a program needn't handle non-finite values.
Results may differ from the reference program's by a relative error of at most 0.0003.
Values sent between devices are 32-bit elements; how exact they have to be, the bound alone decides.
No kernel may reach another device: no remote copies, remote signals or barrier semaphores. Data moves between devices by JAX's collectives and lax.ppermute only.
A program may use at most 128 MiB of HBM per device.

```python
import math
import jax
import jax.numpy as jnp
from jax import lax

ENS = 64
COLS = 128
NOBS = 32
SWEEPS = 6
NX = 512
NY = 4096
NYT = 32


def place_ends(array, stream_key, low, largest):
    longest = array.shape.index(max(array.shape))
    spots = []
    for shift in (0, 1):
        where = [jax.random.randint(jax.random.fold_in(stream_key, axis), (), 0, length) for axis, length in enumerate(array.shape)]
        where[longest] = (where[longest] + shift) % array.shape[longest]
        spots.append(tuple(where))
    return array.at[spots[0]].set(low).at[spots[1]].set(largest)


def level_of(key, extent, split, low, high):
    gain, own = 1.0, jax.random.fold_in(key, 6)
    for axis_at, shards_of in split:
        heights = jnp.exp(jax.random.uniform(jax.random.fold_in(own, axis_at), (shards_of,), jnp.float32, low / len(split), high / len(split)))
        gain = gain * jnp.repeat(heights, extent[axis_at] // shards_of).reshape([-1 if axis == axis_at else 1 for axis in range(len(extent))])
    return gain


def noise(rng, extent, width, limit, pieces=(), held_as=jnp.bfloat16):
    entries = jax.random.normal(rng, extent, jnp.float32) * width
    if len(pieces) > 0:
        entries = level_of(rng, extent, pieces, -0.22, 0.18) * entries
    return jnp.clip(entries, min=-limit, max=limit).astype(held_as)


def setup_inputs(seed: int = 0) -> dict:
    streams_of = jax.random.split(jax.random.key(seed), 8)
    ensemble = noise(streams_of[0], (ENS, NX, NY), 1.0, 6.0, ((0, 32), (1, 8)), jnp.float32)
    velocity = jnp.clip(jax.random.uniform(streams_of[1], (2, NX, NY), jnp.float32, -0.45, 0.45) * level_of(streams_of[1], (2, NX, NY), ((1, 8),), -0.4, 0.0), -0.45, 0.45)
    observed_column = place_ends(jax.random.randint(streams_of[2], (NX, NYT, NOBS), 0, COLS), jax.random.fold_in(streams_of[2], 1), 0, COLS - 1).astype(jnp.int32)
    observation_slot_count = place_ends(jax.random.randint(streams_of[3], (NX, NYT), 1, NOBS + 1), jax.random.fold_in(streams_of[3], 1), 1, NOBS).astype(jnp.int32)
    local_radius = place_ends(jax.random.randint(streams_of[4], (NX, NYT), 16, 129), jax.random.fold_in(streams_of[4], 1), 16, 128).astype(jnp.int32)
    observed_value = noise(streams_of[5], (NX, NYT, NOBS), 1.5, 9.0, ((0, 8), (1, 32)), jnp.float32)
    error_variance = jnp.clip(jnp.exp(math.log(2.0) - 2.0794415 * jax.random.uniform(streams_of[6], (NX, NYT, NOBS), jnp.float32) ** level_of(streams_of[6], (NX, NYT, NOBS), ((0, 8), (1, 32)), -0.2, 0.2)), 0.25, 2.0)
    return {"ensemble": ensemble, "velocity": velocity, "observed_column": observed_column, "observation_slot_count": observation_slot_count, "local_radius": local_radius, "observed_value": observed_value, "error_variance": error_variance}


def advect(extended):
    carried_quantity = extended[:-2]
    east_wind = extended[-2]
    north_wind = extended[-1]
    face_x = 0.5 * (east_wind[1:, 1:-1] + east_wind[:-1, 1:-1])
    flux_x = jnp.maximum(face_x, 0.0) * carried_quantity[:, :-1, 1:-1] + jnp.minimum(face_x, 0.0) * carried_quantity[:, 1:, 1:-1]
    face_y = 0.5 * (north_wind[1:-1, 1:] + north_wind[1:-1, :-1])
    flux_y = jnp.maximum(face_y, 0.0) * carried_quantity[:, 1:-1, :-1] + jnp.minimum(face_y, 0.0) * carried_quantity[:, 1:-1, 1:]
    return carried_quantity[:, 1:-1, 1:-1] - (flux_x[:, 1:] - flux_x[:, :-1]) - (flux_y[:, :, 1:] - flux_y[:, :, :-1])

def analyse(background, columns, tally_count, radii, values, variances):
    highest = lax.Precision.HIGHEST
    members = background.shape[0]
    average = lax.optimization_barrier(jnp.mean(background, axis=0))
    anomaly = background - average[None]
    indicator_matrix = (columns[:, :, None] == jnp.arange(COLS, dtype=jnp.int32)[None, None, :]).astype(jnp.float32)
    observed = jnp.einsum('ebc,bsc->ebs', background, indicator_matrix, precision=highest)
    observed_mean = lax.optimization_barrier(jnp.mean(observed, axis=0))
    spread = observed - observed_mean[None]
    slot_index = jnp.arange(columns.shape[1], dtype=jnp.int32)
    active = (slot_index[None, :] < tally_count[:, None]).astype(jnp.float32)
    offset = (columns.astype(jnp.float32) - 0.5 * (COLS - 1)) / radii.astype(jnp.float32)[:, None]
    weight = active / (1.0 + offset * offset) / variances
    scaled = spread * weight[None]
    identity = jnp.eye(members, dtype=jnp.float32)
    system = jnp.einsum('ebs,fbs->bef', scaled, spread, precision=highest) + (members - 1.0) * identity[None]
    frobenius = jnp.sqrt(lax.optimization_barrier(jnp.sum(system * system, axis=(1, 2))))
    root = system / frobenius[:, None, None]
    inverse_root = jnp.broadcast_to(identity, root.shape)
    for number in range(SWEEPS):
        factor = 1.5 * identity[None] - 0.5 * jnp.einsum('bij,bjk->bik', inverse_root, root, precision=highest)
        root = jnp.einsum('bij,bjk->bik', root, factor, precision=highest)
        inverse_root = jnp.einsum('bij,bjk->bik', factor, inverse_root, precision=highest)
    inverse_root = inverse_root / jnp.sqrt(frobenius)[:, None, None]
    innovation = values - observed_mean
    projected = jnp.einsum('ebs,bs->be', scaled, innovation, precision=highest)
    halfway = jnp.einsum('bij,bj->bi', inverse_root, projected, precision=highest)
    mean_weight = jnp.einsum('bij,bj->bi', inverse_root, halfway, precision=highest)
    transform = jnp.sqrt(members - 1.0) * inverse_root + mean_weight[:, :, None]
    return average[None] + jnp.einsum('bkj,kbc->jbc', transform, anomaly, precision=highest)

def reference(ensemble, velocity, observed_column, observation_slot_count, local_radius, observed_value, error_variance):

    def predict_single_member(carried_quantity):
        for number in range(2):
            stacked = jnp.concatenate([carried_quantity[None], velocity], axis=0)
            carried_quantity = advect(jnp.pad(stacked, ((0, 0), (1, 1), (1, 1))))[0]
        return carried_quantity
    predicted_state = lax.map(predict_single_member, ensemble)
    grouped_by_row = jnp.moveaxis(predicted_state, 1, 0)

    def row_step(packed):
        row_state, columns, tally_count, radii, values, variances = packed
        tile_state = row_state.reshape(ENS, NYT, COLS)
        result = analyse(tile_state, columns, tally_count, radii, values, variances)
        return result.reshape(ENS, NY)
    analysed = lax.map(row_step, (grouped_by_row, observed_column, observation_slot_count, local_radius, observed_value, error_variance))
    return jnp.moveaxis(analysed, 0, 1)
```

```python
import functools

import jax
import jax.numpy as jnp
from jax import lax
from jax.experimental import pallas as pl
from jax.experimental.pallas import tpu as pltpu
from jax.sharding import PartitionSpec as P

COLS = 128
SWEEPS = 6
LANE = 128
BLOCK = 1024
GROUP = 4
SLOTS = 32
SIDE = 8


def stencil(window, first_col, last_col, rows_of):
    fields, wind_x, wind_y = window[:-2], window[-2], window[-1]
    rows, lanes = wind_x.shape
    face_x = 0.5 * (wind_x + pltpu.roll(wind_x, rows - 1, 0))
    before_x = pltpu.roll(face_x, 1, 0)
    face_y = 0.5 * (wind_y + pltpu.roll(wind_y, lanes - 1, 1))
    before_y = pltpu.roll(face_y, 1, 1)
    zero = jnp.zeros_like(face_x)
    centre = (
        1.0
        - jnp.maximum(face_x, 0.0)
        + jnp.minimum(before_x, 0.0)
        - jnp.maximum(face_y, 0.0)
        + jnp.minimum(before_y, 0.0)
    )
    row = lax.broadcasted_iota(jnp.int32, face_x.shape, 0)
    col = lax.broadcasted_iota(jnp.int32, face_x.shape, 1)
    low_row, high_row = rows_of
    north = jnp.where(row == low_row, zero, jnp.maximum(before_x, 0.0))
    south = jnp.where(row == high_row, zero, jnp.minimum(face_x, 0.0))
    west = jnp.where(col == first_col, zero, jnp.maximum(before_y, 0.0))
    east = jnp.where(col == last_col, zero, jnp.minimum(face_y, 0.0))
    out = []
    for field in fields:
        for _ in range(2):
            field = (
                centre * field
                + north * pltpu.roll(field, 1, 0)
                - south * pltpu.roll(field, rows - 1, 0)
                + west * pltpu.roll(field, 1, 1)
                - east * pltpu.roll(field, lanes - 1, 1)
            )
        out.append(field)
    return out


def advance(window_ref, out_ref, out_row, kept, low_row, high_row):
    width = window_ref.shape[2] - 2 * LANE
    count = BLOCK // LANE

    def step(k, carry):
        start = pl.multiple_of(k * BLOCK, BLOCK)
        window = [window_ref[i, :, pl.ds(start, BLOCK + 2 * LANE)] for i in range(4)]
        new = stencil(window, LANE - start, LANE - start + width - 1, (low_row, high_row))
        for m, field in enumerate(new):
            for t in range(count):
                out_ref[k * count + t, m, pl.ds(out_row, kept), :] = field[
                    SIDE : SIDE + kept, LANE * (t + 1) : LANE * (t + 2)
                ]
        return carry

    lax.fori_loop(0, width // BLOCK, step, 0)


def inner_kernel(ensemble_ref, velocity_ref, out_ref, window_ref, *, row0, kept):
    width = ensemble_ref.shape[2]
    rows = kept + 2 * SIDE
    pad = jnp.zeros((4, rows, LANE), jnp.float32)
    window_ref[:, :, pl.ds(0, LANE)] = pad
    window_ref[:, :, pl.ds(LANE + width, LANE)] = pad
    for i in range(2):
        window_ref[i, :, pl.ds(LANE, width)] = ensemble_ref[i, pl.ds(row0 - SIDE, rows), :]
        window_ref[2 + i, :, pl.ds(LANE, width)] = velocity_ref[i, pl.ds(row0 - SIDE, rows), :]
    advance(window_ref, out_ref, 0, kept, -1, -1)


def edge_kernel(edge_ref, ensemble_ref, velocity_ref, above_ref, below_ref, out_ref, window_ref, *, kept):
    height, width = ensemble_ref.shape[1:]
    rows = kept + 2 * SIDE
    pad = jnp.zeros((4, rows, LANE), jnp.float32)
    window_ref[:, :, pl.ds(0, LANE)] = pad
    window_ref[:, :, pl.ds(LANE + width, LANE)] = pad
    span = pl.ds(LANE, width)
    window_ref[:, pl.ds(0, SIDE), span] = jnp.zeros((4, SIDE, width), jnp.float32)
    window_ref[:, pl.ds(SIDE - 2, 2), span] = above_ref[...]
    for i in range(2):
        window_ref[i, pl.ds(SIDE, rows - SIDE), span] = ensemble_ref[i, pl.ds(0, rows - SIDE), :]
        window_ref[2 + i, pl.ds(SIDE, rows - SIDE), span] = velocity_ref[i, pl.ds(0, rows - SIDE), :]
    advance(window_ref, out_ref, 0, kept, jnp.where(edge_ref[0] == 1, SIDE, -1), -1)
    window_ref[:, pl.ds(rows - SIDE, SIDE), span] = jnp.zeros((4, SIDE, width), jnp.float32)
    window_ref[:, pl.ds(rows - SIDE, 2), span] = below_ref[...]
    first = height - (rows - SIDE)
    for i in range(2):
        window_ref[i, pl.ds(0, rows - SIDE), span] = ensemble_ref[i, pl.ds(first, rows - SIDE), :]
        window_ref[2 + i, pl.ds(0, rows - SIDE), span] = velocity_ref[i, pl.ds(first, rows - SIDE), :]
    advance(window_ref, out_ref, kept, kept, -1, jnp.where(edge_ref[1] == 1, SIDE + kept - 1, -1))


def vmem():
    return pl.BlockSpec(memory_space=pltpu.VMEM)


def forecast_inner(ensemble, velocity, row0, kept):
    members, _, width = ensemble.shape
    return pl.pallas_call(
        functools.partial(inner_kernel, row0=row0, kept=kept),
        out_shape=jax.ShapeDtypeStruct((width // COLS, members, kept, COLS), jnp.float32),
        in_specs=[vmem(), vmem()],
        out_specs=vmem(),
        scratch_shapes=[pltpu.VMEM((4, kept + 2 * SIDE, width + 2 * LANE), jnp.float32)],
        name="forecast_inner",
    )(ensemble, velocity)


def forecast_edge(edges, ensemble, velocity, above, below, kept):
    members, _, width = ensemble.shape
    return pl.pallas_call(
        functools.partial(edge_kernel, kept=kept),
        out_shape=jax.ShapeDtypeStruct((width // COLS, members, 2 * kept, COLS), jnp.float32),
        in_specs=[pl.BlockSpec(memory_space=pltpu.SMEM), vmem(), vmem(), vmem(), vmem()],
        out_specs=vmem(),
        scratch_shapes=[pltpu.VMEM((4, kept + 2 * SIDE, width + 2 * LANE), jnp.float32)],
        name="forecast_edge",
    )(edges, ensemble, velocity, above, below)


def split(x, parts=2):
    out = []
    for _ in range(parts - 1):
        out.append(x.astype(jnp.bfloat16))
        x = x - out[-1].astype(jnp.float32)
    return [*out, x.astype(jnp.bfloat16)]


def mm(a, b, dim=0):
    return lax.dot_general(a, b, (((1,), (dim,)), ((), ())), preferred_element_type=jnp.float32)


def product(left, right, dim=0):
    rows = left[0].shape[0]
    total = None
    for i in reversed(range(len(right))):
        kept = left[: len(right) - i]
        both = mm(jnp.concatenate(kept, axis=0), right[i], dim)
        for j in reversed(range(len(kept))):
            part = both[rows * j : rows * (j + 1)]
            total = part if total is None else total + part
    return total


def times(left, right):
    return product(split(left, len(right)), right)


def tile_of(ref, tile):
    members, tiles, width = ref.shape
    return ref.reshape(members * tiles, width).at[pl.ds(tile, members, stride=tiles), :]


def analysis_kernel(col_ref, root_ref, value_ref, x_ref, out_ref, *, groups):
    members = x_ref.shape[0]
    spare = members - 1.0
    wide = GROUP * members
    lane = lax.broadcasted_iota(jnp.int32, (1, LANE), 1)
    slots_of = [(lane // SLOTS) == b for b in range(GROUP)]

    def indicator(shape, row_size, col_size):
        row = lax.broadcasted_iota(jnp.int32, shape, 0) // row_size
        col = lax.broadcasted_iota(jnp.int32, shape, 1) // col_size
        return jnp.where(row == col, 1.0, 0.0).astype(jnp.bfloat16)

    block = indicator((wide, wide), members, members)
    slot_block = indicator((wide, LANE), members, SLOTS)
    eye = jnp.where(
        lax.broadcasted_iota(jnp.int32, (members, wide), 0)
        == lax.broadcasted_iota(jnp.int32, (members, wide), 1) % members,
        1.0,
        0.0,
    )
    spare_rows = jnp.zeros((15, wide), jnp.float32)

    def stacked(parts, mask):
        return [jnp.concatenate([part] * GROUP, axis=0) * mask for part in parts]

    def one(g):
        averages, anomalies = [], []
        spread = jnp.zeros((members, LANE), jnp.float32)
        there = jnp.zeros((8, LANE), jnp.float32)
        index = jnp.broadcast_to(col_ref[pl.ds(g, 1), :], (members, LANE))
        for b in range(GROUP):
            x = tile_of(x_ref, g * GROUP + b)[...]
            average = jnp.mean(x, axis=0, keepdims=True)
            anomaly = x - average
            averages.append(average)
            anomalies.append(anomaly)
            seen = jnp.take_along_axis(anomaly, index, axis=1, mode="promise_in_bounds")
            spread = jnp.where(slots_of[b], seen, spread)
            mean_seen = jnp.take_along_axis(
                jnp.broadcast_to(average, (8, LANE)), index[:8], axis=1, mode="promise_in_bounds"
            )
            there = jnp.where(slots_of[b], mean_seen, there)
        root = root_ref[pl.ds(g, 1), :]
        scaled = spread * root
        innovation = root * (value_ref[pl.ds(g, 1), :] - there[:1])
        yield
        scaled_split = split(scaled)
        wanted = jnp.concatenate([innovation, spare_rows[:, :LANE]], axis=0)
        left = [jnp.concatenate(pair, axis=0) for pair in zip(scaled_split, split(wanted))]
        stage = product(left, stacked(scaled_split, slot_block), 1)
        system = stage[:members] + spare * eye
        wanted = stage[members:]
        yield
        squares = jnp.sum(system * system, axis=0, keepdims=True)
        pieces = split(squares, 3) + [jnp.zeros((13, wide), jnp.bfloat16)]
        total = jnp.sum(mm(jnp.concatenate(pieces, axis=0), block), axis=0, keepdims=True)
        yield
        inverse = 1.0 / jnp.sqrt(total)
        root_norm = jnp.sqrt(inverse)
        system = system * inverse
        result = None
        for number in range(SWEEPS):
            factor = 1.5 * eye - 0.5 * system
            right = stacked(split(factor), block)
            last = number == SWEEPS - 1
            if last:
                stage = times(jnp.concatenate([result, wanted], axis=0), right)
                result, wanted = stage[:members], stage[members:]
            elif number == 0:
                stage = times(jnp.concatenate([system, wanted], axis=0), right)
                result, wanted = factor, stage[members:]
            else:
                stage = times(jnp.concatenate([system, result, wanted], axis=0), right)
                result, wanted = stage[members : 2 * members], stage[2 * members :]
            yield
            if not last:
                system = times(stage[:members], right)
                yield
        mean_weight = times(wanted, stacked(split(result), block))[:1] * inverse
        yield
        gain = split((spare**0.5 * root_norm) * result + mean_weight)
        high, low = split(jnp.concatenate(anomalies, axis=0))
        part = product(stacked(gain, block), [high, low])
        for b in range(GROUP):
            tile_of(out_ref, g * GROUP + b)[...] = part[members * b : members * (b + 1)] + averages[b]
        yield

    running = [one(g) for g in range(groups)]
    while running:
        running = [r for r in running if next(r, running) is None]


def analyse(background, columns, root_weight, values, groups):
    members, rows, width = background.shape
    tiles = groups * GROUP
    packed = lambda a: a.reshape(rows // tiles, groups, LANE)
    spec = pl.BlockSpec((None, groups, LANE), lambda i: (i, 0, 0))
    field = pl.BlockSpec((members, tiles, width), lambda i: (0, i, 0))
    return pl.pallas_call(
        functools.partial(analysis_kernel, groups=groups),
        grid=(rows // tiles,),
        out_shape=jax.ShapeDtypeStruct(background.shape, jnp.float32),
        in_specs=[spec, spec, spec, field],
        out_specs=field,
        name="analysis",
    )(packed(columns), packed(root_weight), packed(values), background)


def exchange(x):
    return lax.all_to_all(x, "member", 0, 0, tiled=True)


def per_device(ensemble, velocity, observed_column, slot_count, radius, observed_value, error_variance):
    members, height, width = ensemble.shape
    devices = lax.axis_size("tile")
    here = lax.axis_index("tile")
    edges = jnp.stack([here == 0, here == devices - 1]).astype(jnp.int32)
    up = [(i, i + 1) for i in range(devices - 1)]
    down = [(j, i) for i, j in up]
    above = lax.ppermute(
        jnp.concatenate([ensemble[:, -2:], velocity[:, -2:]], axis=0), "tile", up
    )
    below = lax.ppermute(jnp.concatenate([ensemble[:, :2], velocity[:, :2]], axis=0), "tile", down)

    columns = observed_column[:, 0]
    values = observed_value[:, 0]
    active = (jnp.arange(SLOTS, dtype=jnp.int32)[None, :] < slot_count).astype(jnp.float32)
    offset = (columns.astype(jnp.float32) - 0.5 * (COLS - 1)) / radius.astype(jnp.float32)
    root_weight = jnp.sqrt(active / (1.0 + offset * offset) / error_variance[:, 0])

    edge = height // 4
    kept = height - 2 * edge
    inner = slice(edge, height - edge)
    outer = lambda a, axis: jnp.concatenate(
        [lax.slice_in_dim(a, 0, edge, axis=axis), lax.slice_in_dim(a, height - edge, height, axis=axis)],
        axis=axis,
    )
    first = forecast_inner(ensemble, velocity, edge, kept)
    first, above, below = lax.optimization_barrier((first, above, below))
    first = exchange(first.reshape(-1, kept, COLS))
    second = exchange(forecast_edge(edges, ensemble, velocity, above, below, edge).reshape(-1, 2 * edge, COLS))
    first = analyse(first, columns[inner], root_weight[inner], values[inner], 2)
    first = exchange(first)
    second = analyse(second, outer(columns, 0), outer(root_weight, 0), outer(values, 0), 2)
    second = exchange(second)
    both = jnp.concatenate([second[:, :edge], first, second[:, edge:]], axis=1)
    both = both.reshape(-1, members, height, COLS)
    return both.transpose(1, 2, 0, 3).reshape(members, height, width)


def solution(mesh):
    return jax.shard_map(
        per_device,
        mesh=mesh,
        in_specs=(
            P("member", "tile", None),
            P(None, "tile", None),
            P("tile", "member", None),
            P("tile", "member"),
            P("tile", "member"),
            P("tile", "member", None),
            P("tile", "member", None),
        ),
        out_specs=P("member", "tile", None),
        check_vma=False,
    )
```

```python
import functools

import jax
import jax.numpy as jnp
from jax import lax
from jax.experimental import pallas as pl
from jax.experimental.pallas import tpu as pltpu
from jax.sharding import PartitionSpec as P

COLS = 128
SWEEPS = 6
LANE = 128
BLOCK = 2048
GROUP = 4
SLOTS = 32
SIDE = 8


def stencil(fields, wind_x, wind_y, first_col, last_col, low_row, high_row):
    rows, lanes = wind_x.shape
    face_x = 0.5 * (wind_x + pltpu.roll(wind_x, rows - 1, 0))
    before_x = pltpu.roll(face_x, 1, 0)
    face_y = 0.5 * (wind_y + pltpu.roll(wind_y, lanes - 1, 1))
    before_y = pltpu.roll(face_y, 1, 1)
    zero = jnp.zeros_like(face_x)
    centre = (
        1.0
        - jnp.maximum(face_x, 0.0)
        + jnp.minimum(before_x, 0.0)
        - jnp.maximum(face_y, 0.0)
        + jnp.minimum(before_y, 0.0)
    )
    north, south = jnp.maximum(before_x, 0.0), jnp.minimum(face_x, 0.0)
    row = lax.broadcasted_iota(jnp.int32, face_x.shape, 0)
    if low_row is not None:
        north = jnp.where(row == low_row, zero, north)
    if high_row is not None:
        south = jnp.where(row == high_row, zero, south)
    col = lax.broadcasted_iota(jnp.int32, face_x.shape, 1)
    west = jnp.where(col == first_col, zero, jnp.maximum(before_y, 0.0))
    east = jnp.where(col == last_col, zero, jnp.minimum(face_y, 0.0))

    def substep(field, part):
        return (
            centre[part] * field[part]
            + north[part] * pltpu.roll(field, 1, 0)[part]
            - south[part] * pltpu.roll(field, rows - 1, 0)[part]
            + west[part] * pltpu.roll(field, 1, 1)[part]
            - east[part] * pltpu.roll(field, lanes - 1, 1)[part]
        )

    kept = (slice(SIDE, rows - SIDE), slice(LANE, lanes - LANE))
    return [substep(substep(field, (slice(None), slice(None))), kept) for field in fields]


def advance(pieces, out_ref, out_row, low_row, high_row):
    k, last = pl.program_id(0), pl.num_programs(0) - 1
    *fields, wind_x, wind_y = pieces
    rows, lanes = wind_x.shape
    inside_left = jnp.where(k > 0, wind_y[:, :LANE], 0.0)
    inside_right = jnp.where(k < last, wind_y[:, lanes - LANE :], 0.0)
    wind_y = jnp.concatenate([inside_left, wind_y[:, LANE : lanes - LANE], inside_right], axis=1)
    first_col = jnp.where(k == 0, LANE, -1)
    last_col = jnp.where(k == last, lanes - LANE - 1, -1)
    new = stencil(fields, wind_x, wind_y, first_col, last_col, low_row, high_row)
    for m, field in enumerate(new):
        for t in range(field.shape[1] // LANE):
            out_ref[t, m, pl.ds(out_row, rows - 2 * SIDE), :] = field[:, LANE * t : LANE * (t + 1)]


def joined(refs, i, rows):
    return jnp.concatenate([ref[i, rows, :] for ref in refs], axis=1)


def inner_kernel(*refs, row0, kept):
    *refs, out_ref = refs
    rows = slice(row0 - SIDE, row0 + kept + SIDE)
    advance([joined(refs[3 * (i // 2) : 3 * (i // 2) + 3], i % 2, rows) for i in range(4)], out_ref, 0, None, None)


def edge_kernel(edge_ref, *refs, kept):
    *refs, out_ref = refs
    height = refs[0].shape[1]
    far = jnp.zeros((SIDE - 2, out_ref.shape[0] * LANE + 2 * LANE), jnp.float32)
    body = lambda i, rows: joined(refs[3 * (i // 2) : 3 * (i // 2) + 3], i % 2, rows)
    beyond = lambda j, i: joined(refs[6 + 3 * j : 9 + 3 * j], i, slice(None))
    top = [
        jnp.concatenate([far, beyond(0, i), body(i, slice(0, kept + SIDE))], axis=0) for i in range(4)
    ]
    advance(top, out_ref, 0, jnp.where(edge_ref[0] == 1, SIDE, -1), None)
    bottom = [
        jnp.concatenate([body(i, slice(height - kept - SIDE, height)), beyond(1, i), far], axis=0)
        for i in range(4)
    ]
    advance(bottom, out_ref, kept, None, jnp.where(edge_ref[1] == 1, SIDE + kept - 1, -1))


def around(count, height, width):
    per, last = BLOCK // LANE, width // LANE - 1
    return [
        pl.BlockSpec((count, height, LANE), lambda k: (0, 0, jnp.maximum(per * k - 1, 0))),
        pl.BlockSpec((count, height, BLOCK), lambda k: (0, 0, k)),
        pl.BlockSpec((count, height, LANE), lambda k: (0, 0, jnp.minimum(per * (k + 1), last))),
    ]


def forecast_inner(ensemble, velocity, row0, kept):
    members, height, width = ensemble.shape
    per = BLOCK // LANE
    return pl.pallas_call(
        functools.partial(inner_kernel, row0=row0, kept=kept),
        grid=(width // BLOCK,),
        out_shape=jax.ShapeDtypeStruct((width // COLS, members, kept, COLS), jnp.float32),
        in_specs=around(members, height, width) + around(2, height, width),
        out_specs=pl.BlockSpec((per, members, kept, COLS), lambda k: (k, 0, 0, 0)),
        name="forecast_inner",
    )(*[ensemble] * 3, *[velocity] * 3)


def forecast_edge(edges, ensemble, velocity, above, below, kept):
    members, height, width = ensemble.shape
    per = BLOCK // LANE
    return pl.pallas_call(
        functools.partial(edge_kernel, kept=kept),
        grid=(width // BLOCK,),
        out_shape=jax.ShapeDtypeStruct((width // COLS, members, 2 * kept, COLS), jnp.float32),
        in_specs=[pl.BlockSpec(memory_space=pltpu.SMEM)]
        + around(members, height, width)
        + around(2, height, width)
        + around(4, 2, width) * 2,
        out_specs=pl.BlockSpec((per, members, 2 * kept, COLS), lambda k: (k, 0, 0, 0)),
        name="forecast_edge",
    )(edges, *[ensemble] * 3, *[velocity] * 3, *[above] * 3, *[below] * 3)


def split(x, parts=2):
    out = []
    for _ in range(parts - 1):
        out.append(x.astype(jnp.bfloat16))
        x = x - out[-1].astype(jnp.float32)
    return [*out, x.astype(jnp.bfloat16)]


def mm(a, b, dim=0):
    return lax.dot_general(a, b, (((1,), (dim,)), ((), ())), preferred_element_type=jnp.float32)


def product(left, right, dim=0):
    rows = left[0].shape[0]
    total = None
    for i in reversed(range(len(right))):
        kept = left[: len(right) - i]
        both = mm(jnp.concatenate(kept, axis=0), right[i], dim)
        for j in reversed(range(len(kept))):
            part = both[rows * j : rows * (j + 1)]
            total = part if total is None else total + part
    return total


def times(left, right):
    return product(split(left, len(right)), right)


def tile_of(ref, tile):
    members, tiles, width = ref.shape
    return ref.reshape(members * tiles, width).at[pl.ds(tile, members, stride=tiles), :]


def analysis_kernel(col_ref, root_ref, value_ref, x_ref, out_ref, *, groups):
    members = x_ref.shape[0]
    spare = members - 1.0
    wide = GROUP * members
    lane = lax.broadcasted_iota(jnp.int32, (1, LANE), 1)
    slots_of = [(lane // SLOTS) == b for b in range(GROUP)]

    def indicator(shape, row_size, col_size):
        row = lax.broadcasted_iota(jnp.int32, shape, 0) // row_size
        col = lax.broadcasted_iota(jnp.int32, shape, 1) // col_size
        return jnp.where(row == col, 1.0, 0.0).astype(jnp.bfloat16)

    block = indicator((wide, wide), members, members)
    slot_block = indicator((wide, LANE), members, SLOTS)
    eye = jnp.where(
        lax.broadcasted_iota(jnp.int32, (members, wide), 0)
        == lax.broadcasted_iota(jnp.int32, (members, wide), 1) % members,
        1.0,
        0.0,
    )
    spare_rows = jnp.zeros((15, wide), jnp.float32)

    def stacked(parts, mask):
        return [jnp.concatenate([part] * GROUP, axis=0) * mask for part in parts]

    def one(g):
        averages, anomalies = [], []
        spread = jnp.zeros((members, LANE), jnp.float32)
        there = jnp.zeros((8, LANE), jnp.float32)
        index = jnp.broadcast_to(col_ref[pl.ds(g, 1), :], (members, LANE))
        for b in range(GROUP):
            x = tile_of(x_ref, g * GROUP + b)[...]
            average = jnp.mean(x, axis=0, keepdims=True)
            anomaly = x - average
            averages.append(average)
            anomalies.append(anomaly)
            seen = jnp.take_along_axis(anomaly, index, axis=1, mode="promise_in_bounds")
            spread = jnp.where(slots_of[b], seen, spread)
            mean_seen = jnp.take_along_axis(
                jnp.broadcast_to(average, (8, LANE)), index[:8], axis=1, mode="promise_in_bounds"
            )
            there = jnp.where(slots_of[b], mean_seen, there)
        root = root_ref[pl.ds(g, 1), :]
        scaled = spread * root
        innovation = root * (value_ref[pl.ds(g, 1), :] - there[:1])
        yield
        scaled_split = split(scaled)
        wanted = jnp.concatenate([innovation, spare_rows[:, :LANE]], axis=0)
        left = [jnp.concatenate(pair, axis=0) for pair in zip(scaled_split, split(wanted))]
        stage = product(left, stacked(scaled_split, slot_block), 1)
        system = stage[:members] + spare * eye
        wanted = stage[members:]
        yield
        squares = jnp.sum(system * system, axis=0, keepdims=True)
        pieces = split(squares, 3) + [jnp.zeros((13, wide), jnp.bfloat16)]
        total = jnp.sum(mm(jnp.concatenate(pieces, axis=0), block), axis=0, keepdims=True)
        yield
        inverse = 1.0 / jnp.sqrt(total)
        root_norm = jnp.sqrt(inverse)
        system = system * inverse
        result = None
        for number in range(SWEEPS):
            factor = 1.5 * eye - 0.5 * system
            right = stacked(split(factor), block)
            last = number == SWEEPS - 1
            if last:
                stage = times(jnp.concatenate([result, wanted], axis=0), right)
                result, wanted = stage[:members], stage[members:]
            elif number == 0:
                stage = times(jnp.concatenate([system, wanted], axis=0), right)
                result, wanted = factor, stage[members:]
            else:
                stage = times(jnp.concatenate([system, result, wanted], axis=0), right)
                result, wanted = stage[members : 2 * members], stage[2 * members :]
            yield
            if not last:
                system = times(stage[:members], right)
                yield
        mean_weight = times(wanted, stacked(split(result), block))[:1] * inverse
        yield
        gain = split((spare**0.5 * root_norm) * result + mean_weight)
        high, low = split(jnp.concatenate(anomalies, axis=0))
        part = product(stacked(gain, block), [high, low])
        for b in range(GROUP):
            tile_of(out_ref, g * GROUP + b)[...] = part[members * b : members * (b + 1)] + averages[b]
        yield

    running = [one(g) for g in range(groups)]
    while running:
        running = [r for r in running if next(r, running) is None]


def analyse(background, observations, groups, total, first_block, earlier=None):
    members, rows, width = background.shape
    tiles = groups * GROUP
    packed = [a.reshape(rows // tiles, groups, LANE) for a in observations]
    spec = pl.BlockSpec((None, groups, LANE), lambda i: (i, 0, 0))
    field = lambda shift: pl.BlockSpec((members, tiles, width), lambda i: (0, i + shift, 0))
    kernel = functools.partial(analysis_kernel, groups=groups)
    more = {}
    if earlier is not None:
        inner = kernel
        kernel = lambda a, b, c, x, _, out: inner(a, b, c, x, out)
        more = {"input_output_aliases": {4: 0}}
    return pl.pallas_call(
        kernel,
        grid=(rows // tiles,),
        out_shape=jax.ShapeDtypeStruct((members, total, width), jnp.float32),
        in_specs=[spec, spec, spec, field(0)] + [pl.BlockSpec(memory_space=pl.ANY)] * len(more),
        out_specs=field(first_block),
        name="analysis",
        **more,
    )(*packed, background, *([] if earlier is None else [earlier]))


def exchange(x):
    return lax.all_to_all(x, "member", 0, 0, tiled=True)


def per_device(ensemble, velocity, observed_column, slot_count, radius, observed_value, error_variance):
    members, height, width = ensemble.shape
    devices = lax.axis_size("tile")
    here = lax.axis_index("tile")
    up = [(i, i + 1) for i in range(devices - 1)]
    down = [(j, i) for i, j in up]
    edge = height // 8
    kept = height - 2 * edge
    blocks = kept // (4 * GROUP)
    inner = slice(edge, height - edge)
    outer = lambda a, axis: jnp.concatenate(
        [lax.slice_in_dim(a, 0, edge, axis=axis), lax.slice_in_dim(a, height - edge, height, axis=axis)],
        axis=axis,
    )
    columns = observed_column[:, 0]
    values = observed_value[:, 0]
    active = (jnp.arange(SLOTS, dtype=jnp.int32)[None, :] < slot_count).astype(jnp.float32)
    offset = (columns.astype(jnp.float32) - 0.5 * (COLS - 1)) / radius.astype(jnp.float32)
    root_weight = jnp.sqrt(active / (1.0 + offset * offset) / error_variance[:, 0])
    inner_obs = [a[inner] for a in (columns, root_weight, values)]
    outer_obs = [outer(a, 0) for a in (columns, root_weight, values)]
    edges = jnp.stack([here == 0, here == devices - 1]).astype(jnp.int32)

    first = forecast_inner(ensemble, velocity, edge, kept)
    first = exchange(first.reshape(-1, kept, COLS))
    above = lax.ppermute(jnp.concatenate([ensemble[:, -2:], velocity[:, -2:]], axis=0), "tile", up)
    below = lax.ppermute(jnp.concatenate([ensemble[:, :2], velocity[:, :2]], axis=0), "tile", down)
    second = forecast_edge(edges, ensemble, velocity, above, below, edge)
    second = exchange(second.reshape(-1, 2 * edge, COLS))
    done = analyse(first, inner_obs, 4, height, 0)
    done = analyse(second, outer_obs, 4, height, blocks, done)
    done = exchange(done)
    both = jnp.concatenate([done[:, kept : kept + edge], done[:, :kept], done[:, kept + edge :]], axis=1)
    both = both.reshape(-1, members, height, COLS)
    return both.transpose(1, 2, 0, 3).reshape(members, height, width)


def solution(mesh):
    return jax.shard_map(
        per_device,
        mesh=mesh,
        in_specs=(
            P("member", "tile", None),
            P(None, "tile", None),
            P("tile", "member", None),
            P("tile", "member"),
            P("tile", "member"),
            P("tile", "member", None),
            P("tile", "member", None),
        ),
        out_specs=P("member", "tile", None),
        check_vma=False,
    )
```

```python
import functools

import jax
import jax.numpy as jnp
from jax import lax
from jax.experimental import pallas as pl
from jax.experimental.pallas import tpu as pltpu
from jax.sharding import PartitionSpec as P

COLS = 128
SWEEPS = 6
LANE = 128
BLOCK = 2048
GROUP = 4
SLOTS = 32
SIDE = 8


def stencil(fields, wind_x, wind_y, first_col, last_col, low_row, high_row):
    rows, lanes = wind_x.shape
    face_x = 0.5 * (wind_x + pltpu.roll(wind_x, rows - 1, 0))
    before_x = pltpu.roll(face_x, 1, 0)
    face_y = 0.5 * (wind_y + pltpu.roll(wind_y, lanes - 1, 1))
    before_y = pltpu.roll(face_y, 1, 1)
    zero = jnp.zeros_like(face_x)
    centre = (
        1.0
        - jnp.maximum(face_x, 0.0)
        + jnp.minimum(before_x, 0.0)
        - jnp.maximum(face_y, 0.0)
        + jnp.minimum(before_y, 0.0)
    )
    north, south = jnp.maximum(before_x, 0.0), jnp.minimum(face_x, 0.0)
    row = lax.broadcasted_iota(jnp.int32, face_x.shape, 0)
    if low_row is not None:
        north = jnp.where(row == low_row, zero, north)
    if high_row is not None:
        south = jnp.where(row == high_row, zero, south)
    col = lax.broadcasted_iota(jnp.int32, face_x.shape, 1)
    west = jnp.where(col == first_col, zero, jnp.maximum(before_y, 0.0))
    east = jnp.where(col == last_col, zero, jnp.minimum(face_y, 0.0))

    def substep(field, part):
        return (
            centre[part] * field[part]
            + north[part] * pltpu.roll(field, 1, 0)[part]
            - south[part] * pltpu.roll(field, rows - 1, 0)[part]
            + west[part] * pltpu.roll(field, 1, 1)[part]
            - east[part] * pltpu.roll(field, lanes - 1, 1)[part]
        )

    kept = (slice(SIDE, rows - SIDE), slice(LANE, lanes - LANE))
    return [substep(substep(field, (slice(None), slice(None))), kept) for field in fields]


def advance(pieces, out_ref, out_row, low_row, high_row):
    k, last = pl.program_id(0), pl.num_programs(0) - 1
    *fields, wind_x, wind_y = pieces
    rows, lanes = wind_x.shape
    inside_left = jnp.where(k > 0, wind_y[:, :LANE], 0.0)
    inside_right = jnp.where(k < last, wind_y[:, lanes - LANE :], 0.0)
    wind_y = jnp.concatenate([inside_left, wind_y[:, LANE : lanes - LANE], inside_right], axis=1)
    first_col = jnp.where(k == 0, LANE, -1)
    last_col = jnp.where(k == last, lanes - LANE - 1, -1)
    new = stencil(fields, wind_x, wind_y, first_col, last_col, low_row, high_row)
    for m, field in enumerate(new):
        for t in range(field.shape[1] // LANE):
            out_ref[t, m, pl.ds(out_row, rows - 2 * SIDE), :] = field[:, LANE * t : LANE * (t + 1)]


def joined(refs, i, rows):
    return jnp.concatenate([ref[i, rows, :] for ref in refs], axis=1)


def inner_kernel(*refs, row0, kept):
    *refs, out_ref = refs
    rows = slice(row0 - SIDE, row0 + kept + SIDE)
    advance([joined(refs[3 * (i // 2) : 3 * (i // 2) + 3], i % 2, rows) for i in range(4)], out_ref, 0, None, None)


def edge_kernel(edge_ref, *refs, kept):
    *refs, out_ref = refs
    height = refs[0].shape[1]
    far = jnp.zeros((SIDE - 2, out_ref.shape[0] * LANE + 2 * LANE), jnp.float32)
    body = lambda i, rows: joined(refs[3 * (i // 2) : 3 * (i // 2) + 3], i % 2, rows)
    beyond = lambda j, i: joined(refs[6 + 3 * j : 9 + 3 * j], i, slice(None))
    top = [
        jnp.concatenate([far, beyond(0, i), body(i, slice(0, kept + SIDE))], axis=0) for i in range(4)
    ]
    advance(top, out_ref, 0, jnp.where(edge_ref[0] == 1, SIDE, -1), None)
    bottom = [
        jnp.concatenate([body(i, slice(height - kept - SIDE, height)), beyond(1, i), far], axis=0)
        for i in range(4)
    ]
    advance(bottom, out_ref, kept, None, jnp.where(edge_ref[1] == 1, SIDE + kept - 1, -1))


def around(count, height, width):
    per, last = BLOCK // LANE, width // LANE - 1
    return [
        pl.BlockSpec((count, height, LANE), lambda k: (0, 0, jnp.maximum(per * k - 1, 0))),
        pl.BlockSpec((count, height, BLOCK), lambda k: (0, 0, k)),
        pl.BlockSpec((count, height, LANE), lambda k: (0, 0, jnp.minimum(per * (k + 1), last))),
    ]


def forecast_inner(ensemble, velocity, row0, kept):
    members, height, width = ensemble.shape
    per = BLOCK // LANE
    return pl.pallas_call(
        functools.partial(inner_kernel, row0=row0, kept=kept),
        grid=(width // BLOCK,),
        out_shape=jax.ShapeDtypeStruct((width // COLS, members, kept, COLS), jnp.float32),
        in_specs=around(members, height, width) + around(2, height, width),
        out_specs=pl.BlockSpec((per, members, kept, COLS), lambda k: (k, 0, 0, 0)),
        name="forecast_inner",
    )(*[ensemble] * 3, *[velocity] * 3)


def forecast_edge(edges, ensemble, velocity, above, below, kept):
    members, height, width = ensemble.shape
    per = BLOCK // LANE
    return pl.pallas_call(
        functools.partial(edge_kernel, kept=kept),
        grid=(width // BLOCK,),
        out_shape=jax.ShapeDtypeStruct((width // COLS, members, 2 * kept, COLS), jnp.float32),
        in_specs=[pl.BlockSpec(memory_space=pltpu.SMEM)]
        + around(members, height, width)
        + around(2, height, width)
        + around(4, 2, width) * 2,
        out_specs=pl.BlockSpec((per, members, 2 * kept, COLS), lambda k: (k, 0, 0, 0)),
        name="forecast_edge",
    )(edges, *[ensemble] * 3, *[velocity] * 3, *[above] * 3, *[below] * 3)


def split(x, parts=2):
    out = []
    for _ in range(parts - 1):
        out.append(x.astype(jnp.bfloat16))
        x = x - out[-1].astype(jnp.float32)
    return [*out, x.astype(jnp.bfloat16)]


def mm(a, b, dim=0):
    return lax.dot_general(a, b, (((1,), (dim,)), ((), ())), preferred_element_type=jnp.float32)


def product(left, right, dim=0):
    rows = left[0].shape[0]
    total = None
    for i in reversed(range(len(right))):
        kept = left[: len(right) - i]
        both = mm(jnp.concatenate(kept, axis=0), right[i], dim)
        for j in reversed(range(len(kept))):
            part = both[rows * j : rows * (j + 1)]
            total = part if total is None else total + part
    return total


def times(left, right):
    return product(split(left, len(right)), right)


def tile_of(ref, tile):
    members, tiles, width = ref.shape
    return ref.reshape(members * tiles, width).at[pl.ds(tile, members, stride=tiles), :]


def analysis_kernel(obs_ref, x_ref, out_ref, *, groups, row_of):
    members = x_ref.shape[0]
    spare = members - 1.0
    wide = GROUP * members
    lane = lax.broadcasted_iota(jnp.int32, (1, LANE), 1)
    slots_of = [(lane // SLOTS) == b for b in range(GROUP)]

    def indicator(shape, row_size, col_size):
        row = lax.broadcasted_iota(jnp.int32, shape, 0) // row_size
        col = lax.broadcasted_iota(jnp.int32, shape, 1) // col_size
        return jnp.where(row == col, 1.0, 0.0).astype(jnp.bfloat16)

    block = indicator((wide, wide), members, members)
    slot_block = indicator((wide, LANE), members, SLOTS)
    eye = jnp.where(
        lax.broadcasted_iota(jnp.int32, (members, wide), 0)
        == lax.broadcasted_iota(jnp.int32, (members, wide), 1) % members,
        1.0,
        0.0,
    )
    spare_rows = jnp.zeros((15, wide), jnp.float32)

    def stacked(parts, mask):
        return [jnp.concatenate([part] * GROUP, axis=0) * mask for part in parts]

    def one(g):
        averages, anomalies = [], []
        spread = jnp.zeros((members, LANE), jnp.float32)
        there = jnp.zeros((8, LANE), jnp.float32)
        row = pl.ds(row_of(g), 1)
        index = jnp.broadcast_to(obs_ref[0, row, :].astype(jnp.int32), (members, LANE))
        for b in range(GROUP):
            x = tile_of(x_ref, g * GROUP + b)[...]
            average = jnp.mean(x, axis=0, keepdims=True)
            anomaly = x - average
            averages.append(average)
            anomalies.append(anomaly)
            seen = jnp.take_along_axis(anomaly, index, axis=1, mode="promise_in_bounds")
            spread = jnp.where(slots_of[b], seen, spread)
            mean_seen = jnp.take_along_axis(
                jnp.broadcast_to(average, (8, LANE)), index[:8], axis=1, mode="promise_in_bounds"
            )
            there = jnp.where(slots_of[b], mean_seen, there)
        root = obs_ref[1, row, :]
        scaled = spread * root
        innovation = root * (obs_ref[2, row, :] - there[:1])
        yield
        scaled_split = split(scaled)
        wanted = jnp.concatenate([innovation, spare_rows[:, :LANE]], axis=0)
        left = [jnp.concatenate(pair, axis=0) for pair in zip(scaled_split, split(wanted))]
        stage = product(left, stacked(scaled_split, slot_block), 1)
        system = stage[:members] + spare * eye
        wanted = stage[members:]
        yield
        squares = jnp.sum(system * system, axis=0, keepdims=True)
        pieces = split(squares, 3) + [jnp.zeros((13, wide), jnp.bfloat16)]
        total = jnp.sum(mm(jnp.concatenate(pieces, axis=0), block), axis=0, keepdims=True)
        yield
        inverse = 1.0 / jnp.sqrt(total)
        root_norm = jnp.sqrt(inverse)
        system = system * inverse
        result = None
        for number in range(SWEEPS):
            factor = 1.5 * eye - 0.5 * system
            right = stacked(split(factor), block)
            last = number == SWEEPS - 1
            if last:
                stage = times(jnp.concatenate([result, wanted], axis=0), right)
                result, wanted = stage[:members], stage[members:]
            elif number == 0:
                stage = times(jnp.concatenate([system, wanted], axis=0), right)
                result, wanted = factor, stage[members:]
            else:
                stage = times(jnp.concatenate([system, result, wanted], axis=0), right)
                result, wanted = stage[members : 2 * members], stage[2 * members :]
            yield
            if not last:
                system = times(stage[:members], right)
                yield
        mean_weight = times(wanted, stacked(split(result), block))[:1] * inverse
        yield
        gain = split((spare**0.5 * root_norm) * result + mean_weight)
        high, low = split(jnp.concatenate(anomalies, axis=0))
        part = product(stacked(gain, block), [high, low])
        for b in range(GROUP):
            tile_of(out_ref, g * GROUP + b)[...] = part[members * b : members * (b + 1)] + averages[b]
        yield

    running = [one(g) for g in range(groups)]
    while running:
        running = [r for r in running if next(r, running) is None]


def analyse(background, observations, groups, total, first_block, row_of, earlier=None):
    members, rows, width = background.shape
    tiles = groups * GROUP
    field = lambda shift: pl.BlockSpec((members, tiles, width), lambda i: (0, i + shift, 0))
    kernel = functools.partial(analysis_kernel, groups=groups, row_of=row_of)
    more = {}
    if earlier is not None:
        inner = kernel
        kernel = lambda o, x, _, out: inner(o, x, out)
        more = {"input_output_aliases": {2: 0}}
    return pl.pallas_call(
        kernel,
        grid=(rows // tiles,),
        out_shape=jax.ShapeDtypeStruct((members, total, width), jnp.float32),
        in_specs=[pl.BlockSpec(observations.shape, lambda i: (0, 0, 0)), field(0)]
        + [pl.BlockSpec(memory_space=pl.ANY)] * len(more),
        out_specs=field(first_block),
        name="analysis",
        **more,
    )(observations, background, *([] if earlier is None else [earlier]))


def exchange(x):
    return lax.all_to_all(x, "member", 0, 0, tiled=True)


def per_device(ensemble, velocity, observed_column, slot_count, radius, observed_value, error_variance):
    members, height, width = ensemble.shape
    devices = lax.axis_size("tile")
    here = lax.axis_index("tile")
    up = [(i, i + 1) for i in range(devices - 1)]
    down = [(j, i) for i, j in up]
    edge = height // 8
    kept = height - 2 * edge
    blocks = kept // (2 * edge)
    before = edge // GROUP
    groups = 2 * before
    inner_row = lambda g: before + groups * pl.program_id(0) + g
    outer_row = lambda g: g if g < before else height // GROUP - 2 * before + g
    columns = observed_column[:, 0]
    values = observed_value[:, 0]
    active = (jnp.arange(SLOTS, dtype=jnp.int32)[None, :] < slot_count).astype(jnp.float32)
    offset = (columns.astype(jnp.float32) - 0.5 * (COLS - 1)) / radius.astype(jnp.float32)
    root_weight = jnp.sqrt(active / (1.0 + offset * offset) / error_variance[:, 0])
    observations = jnp.stack([columns.astype(jnp.float32), root_weight, values])
    observations = observations.reshape(3, height // GROUP, LANE)
    edges = jnp.stack([here == 0, here == devices - 1]).astype(jnp.int32)

    above = lax.ppermute(jnp.concatenate([ensemble[:, -2:], velocity[:, -2:]], axis=0), "tile", up)
    below = lax.ppermute(jnp.concatenate([ensemble[:, :2], velocity[:, :2]], axis=0), "tile", down)
    first = forecast_inner(ensemble, velocity, edge, kept)
    first = exchange(first.reshape(-1, kept, COLS))
    second = forecast_edge(edges, ensemble, velocity, above, below, edge)
    second = exchange(second.reshape(-1, 2 * edge, COLS))
    done = analyse(first, observations, groups, height, 0, inner_row)
    done = analyse(second, observations, groups, height, blocks, outer_row, done)
    done = exchange(done)
    both = jnp.concatenate([done[:, kept : kept + edge], done[:, :kept], done[:, kept + edge :]], axis=1)
    both = both.reshape(-1, members, height, COLS)
    return both.transpose(1, 2, 0, 3).reshape(members, height, width)


def solution(mesh):
    return jax.shard_map(
        per_device,
        mesh=mesh,
        in_specs=(
            P("member", "tile", None),
            P(None, "tile", None),
            P("tile", "member", None),
            P("tile", "member"),
            P("tile", "member"),
            P("tile", "member", None),
            P("tile", "member", None),
        ),
        out_specs=P("member", "tile", None),
        check_vma=False,
    )
```

```python
import functools

import jax
import jax.numpy as jnp
from jax import lax
from jax.experimental import pallas as pl
from jax.experimental.pallas import tpu as pltpu
from jax.sharding import PartitionSpec as P

COLS = 128
SWEEPS = 6
LANE = 128
BLOCK = 2048
GROUP = 4
SLOTS = 32
SIDE = 8


def stencil(fields, wind_x, wind_y, first_col, last_col, low_row, high_row):
    rows, lanes = wind_x.shape
    face_x = 0.5 * (wind_x + pltpu.roll(wind_x, rows - 1, 0))
    before_x = pltpu.roll(face_x, 1, 0)
    face_y = 0.5 * (wind_y + pltpu.roll(wind_y, lanes - 1, 1))
    before_y = pltpu.roll(face_y, 1, 1)
    zero = jnp.zeros_like(face_x)
    centre = (
        1.0
        - jnp.maximum(face_x, 0.0)
        + jnp.minimum(before_x, 0.0)
        - jnp.maximum(face_y, 0.0)
        + jnp.minimum(before_y, 0.0)
    )
    north, south = jnp.maximum(before_x, 0.0), jnp.minimum(face_x, 0.0)
    row = lax.broadcasted_iota(jnp.int32, face_x.shape, 0)
    if low_row is not None:
        north = jnp.where(row == low_row, zero, north)
    if high_row is not None:
        south = jnp.where(row == high_row, zero, south)
    col = lax.broadcasted_iota(jnp.int32, face_x.shape, 1)
    west = jnp.where(col == first_col, zero, jnp.maximum(before_y, 0.0))
    east = jnp.where(col == last_col, zero, jnp.minimum(face_y, 0.0))

    def substep(field, part):
        return (
            centre[part] * field[part]
            + north[part] * pltpu.roll(field, 1, 0)[part]
            - south[part] * pltpu.roll(field, rows - 1, 0)[part]
            + west[part] * pltpu.roll(field, 1, 1)[part]
            - east[part] * pltpu.roll(field, lanes - 1, 1)[part]
        )

    kept = (slice(SIDE, rows - SIDE), slice(LANE, lanes - LANE))
    return [substep(substep(field, (slice(None), slice(None))), kept) for field in fields]


def advance(pieces, out_ref, out_row, low_row, high_row):
    k, last = pl.program_id(0), pl.num_programs(0) - 1
    *fields, wind_x, wind_y = pieces
    rows, lanes = wind_x.shape
    inside_left = jnp.where(k > 0, wind_y[:, :LANE], 0.0)
    inside_right = jnp.where(k < last, wind_y[:, lanes - LANE :], 0.0)
    wind_y = jnp.concatenate([inside_left, wind_y[:, LANE : lanes - LANE], inside_right], axis=1)
    first_col = jnp.where(k == 0, LANE, -1)
    last_col = jnp.where(k == last, lanes - LANE - 1, -1)
    new = stencil(fields, wind_x, wind_y, first_col, last_col, low_row, high_row)
    for m, field in enumerate(new):
        for t in range(field.shape[1] // LANE):
            out_ref[t, m, pl.ds(out_row, rows - 2 * SIDE), :] = field[:, LANE * t : LANE * (t + 1)]


def joined(refs, i, rows):
    return jnp.concatenate([ref[i, rows, :] for ref in refs], axis=1)


def inner_kernel(*refs, row0, kept):
    *refs, out_ref = refs
    rows = slice(row0 - SIDE, row0 + kept + SIDE)
    advance([joined(refs[3 * (i // 2) : 3 * (i // 2) + 3], i % 2, rows) for i in range(4)], out_ref, 0, None, None)


def edge_kernel(edge_ref, *refs, kept):
    *refs, _, out_ref = refs
    tall = refs[0].shape[1]
    far = jnp.zeros((SIDE - 2, out_ref.shape[0] * LANE + 2 * LANE), jnp.float32)
    body = lambda first, i, rows: joined(refs[first + 3 * (i // 2) : first + 3 * (i // 2) + 3], i % 2, rows)
    beyond = lambda j, i: joined(refs[12 + 3 * j : 15 + 3 * j], i, slice(None))
    top = [
        jnp.concatenate([far, beyond(0, i), body(0, i, slice(0, kept + SIDE))], axis=0) for i in range(4)
    ]
    advance(top, out_ref, 0, jnp.where(edge_ref[0] == 1, SIDE, -1), None)
    bottom = [
        jnp.concatenate([body(6, i, slice(tall - kept - SIDE, tall)), beyond(1, i), far], axis=0)
        for i in range(4)
    ]
    advance(bottom, out_ref, kept, None, jnp.where(edge_ref[1] == 1, SIDE + kept - 1, -1))


def vmem():
    return pl.BlockSpec(memory_space=pltpu.VMEM)


def around(count, height, width, row=0):
    per, last = BLOCK // LANE, width // LANE - 1
    return [
        pl.BlockSpec((count, height, LANE), lambda k: (0, row, jnp.maximum(per * k - 1, 0))),
        pl.BlockSpec((count, height, BLOCK), lambda k: (0, row, k)),
        pl.BlockSpec((count, height, LANE), lambda k: (0, row, jnp.minimum(per * (k + 1), last))),
    ]


def forecast_inner(ensemble, velocity, row0, kept):
    members, height, width = ensemble.shape
    per = BLOCK // LANE
    return pl.pallas_call(
        functools.partial(inner_kernel, row0=row0, kept=kept),
        grid=(width // BLOCK,),
        out_shape=jax.ShapeDtypeStruct((width // COLS, members, height, COLS), jnp.float32),
        in_specs=around(members, height, width) + around(2, height, width),
        out_specs=pl.BlockSpec((per, members, kept, COLS), lambda k: (k, 0, 0, 0)),
        name="forecast_inner",
    )(*[ensemble] * 3, *[velocity] * 3)


def forecast_edge(edges, ensemble, velocity, above, below, kept, partial):
    members, height, width = ensemble.shape
    per = BLOCK // LANE
    tall = kept + SIDE
    both = lambda row: around(members, tall, width, row) + around(2, tall, width, row)
    return pl.pallas_call(
        functools.partial(edge_kernel, kept=kept),
        grid=(width // BLOCK,),
        out_shape=jax.ShapeDtypeStruct(partial.shape, jnp.float32),
        in_specs=[pl.BlockSpec(memory_space=pltpu.SMEM)]
        + both(0)
        + both(height // tall - 1)
        + around(4, 2, width) * 2
        + [pl.BlockSpec(memory_space=pl.ANY)],
        out_specs=pl.BlockSpec((per, members, 2 * kept, COLS), lambda k: (k, 0, height // (2 * kept) - 1, 0)),
        input_output_aliases={19: 0},
        name="forecast_edge",
    )(edges, *([ensemble] * 3 + [velocity] * 3) * 2, *[above] * 3, *[below] * 3, partial)


def split(x, parts=2):
    out = []
    for _ in range(parts - 1):
        out.append(x.astype(jnp.bfloat16))
        x = x - out[-1].astype(jnp.float32)
    return [*out, x.astype(jnp.bfloat16)]


def mm(a, b, dim=0):
    return lax.dot_general(a, b, (((1,), (dim,)), ((), ())), preferred_element_type=jnp.float32)


def product(left, right, dim=0):
    rows = left[0].shape[0]
    total = None
    for i in reversed(range(len(right))):
        kept = left[: len(right) - i]
        both = mm(jnp.concatenate(kept, axis=0), right[i], dim)
        for j in reversed(range(len(kept))):
            part = both[rows * j : rows * (j + 1)]
            total = part if total is None else total + part
    return total


def times(left, right):
    return product(split(left, len(right)), right)


def tile_of(ref, tile):
    members, tiles, width = ref.shape
    return ref.reshape(members * tiles, width).at[pl.ds(tile, members, stride=tiles), :]


def analysis_kernel(obs_ref, x_ref, out_ref, *, groups, row_of):
    members = x_ref.shape[0]
    spare = members - 1.0
    wide = GROUP * members
    lane = lax.broadcasted_iota(jnp.int32, (1, LANE), 1)
    slots_of = [(lane // SLOTS) == b for b in range(GROUP)]

    def indicator(shape, row_size, col_size):
        row = lax.broadcasted_iota(jnp.int32, shape, 0) // row_size
        col = lax.broadcasted_iota(jnp.int32, shape, 1) // col_size
        return jnp.where(row == col, 1.0, 0.0).astype(jnp.bfloat16)

    block = indicator((wide, wide), members, members)
    slot_block = indicator((wide, LANE), members, SLOTS)
    eye = jnp.where(
        lax.broadcasted_iota(jnp.int32, (members, wide), 0)
        == lax.broadcasted_iota(jnp.int32, (members, wide), 1) % members,
        1.0,
        0.0,
    )
    spare_rows = jnp.zeros((15, wide), jnp.float32)
    per = LANE // members
    first_half = lax.broadcasted_iota(jnp.int32, (members, LANE), 1) < members
    first_half16 = jnp.where(first_half, 1.0, 0.0).astype(jnp.bfloat16)
    base = pl.program_id(0) * (groups * GROUP)

    def stacked(parts, mask):
        return [jnp.concatenate([part] * GROUP, axis=0) * mask for part in parts]

    def one(g):
        averages, anomalies = [], []
        spread = jnp.zeros((members, LANE), jnp.float32)
        there = jnp.zeros((8, LANE), jnp.float32)
        row = pl.ds(row_of(g), 1)
        index = jnp.broadcast_to(obs_ref[0, row, :].astype(jnp.int32), (members, LANE))
        for b in range(GROUP):
            x = tile_of(x_ref, base + g * GROUP + b)[...]
            average = jnp.mean(x, axis=0, keepdims=True)
            anomaly = x - average
            averages.append(average)
            anomalies.append(anomaly)
            seen = jnp.take_along_axis(anomaly, index, axis=1, mode="promise_in_bounds")
            spread = jnp.where(slots_of[b], seen, spread)
            mean_seen = jnp.take_along_axis(
                jnp.broadcast_to(average, (8, LANE)), index[:8], axis=1, mode="promise_in_bounds"
            )
            there = jnp.where(slots_of[b], mean_seen, there)
        root = obs_ref[1, row, :]
        scaled = spread * root
        innovation = root * (obs_ref[2, row, :] - there[:1])
        yield
        scaled_split = split(scaled)
        wanted = jnp.concatenate([innovation, spare_rows[:, :LANE]], axis=0)
        left = [jnp.concatenate(pair, axis=0) for pair in zip(scaled_split, split(wanted))]
        stage = product(left, stacked(scaled_split, slot_block), 1)
        system = stage[:members] + spare * eye
        wanted = stage[members:]
        yield
        squares = jnp.sum(system * system, axis=0, keepdims=True)
        pieces = split(squares, 3) + [jnp.zeros((13, wide), jnp.bfloat16)]
        total = jnp.sum(mm(jnp.concatenate(pieces, axis=0), block), axis=0, keepdims=True)
        yield
        inverse = 1.0 / jnp.sqrt(total)
        root_norm = jnp.sqrt(inverse)
        system = system * inverse
        result = None
        for number in range(SWEEPS):
            factor = 1.5 * eye - 0.5 * system
            right = stacked(split(factor), block)
            last = number == SWEEPS - 1
            if last:
                result = times(result, right)
            elif number == 0:
                stage, result = times(system, right), factor
            else:
                stage = times(jnp.concatenate([system, result], axis=0), right)
                result = stage[members:]
            yield
            if not last:
                system = times(stage[:members], right)
                yield
        right = stacked(split(result), block)
        wanted = times(wanted, right)
        yield
        mean_weight = times(wanted, right)[:1] * inverse
        yield
        high, low = split((spare**0.5 * root_norm) * result + mean_weight)
        for b in range(GROUP):
            at = LANE * (b // per)
            here, there_low = high[:, at : at + LANE], low[:, at : at + LANE]
            turned = lambda part: pltpu.roll(part.astype(jnp.float32), members, 1).astype(jnp.bfloat16)
            if b % per:
                left = jnp.where(first_half, turned(here), there_low)
            else:
                left = jnp.where(first_half, here, turned(there_low))
            left = jnp.concatenate([left, left * first_half16], axis=1)
            a_high, a_low = split(anomalies[b])
            right = jnp.concatenate([a_high, a_high, a_low, jnp.zeros_like(a_low)], axis=0)
            tile_of(out_ref, base + g * GROUP + b)[...] = mm(left, right) + averages[b]
        yield

    running = [one(g) for g in range(groups)]
    while running:
        running = [r for r in running if next(r, running) is None]


def analyse(background, observations, groups, row_of):
    _, rows, _ = background.shape
    return pl.pallas_call(
        functools.partial(analysis_kernel, groups=groups, row_of=row_of),
        grid=(rows // (groups * GROUP),),
        out_shape=pltpu.VMEM(background.shape, jnp.float32),
        in_specs=[vmem(), vmem()],
        out_specs=vmem(),
        compiler_params=pltpu.CompilerParams(vmem_limit_bytes=32 << 20),
        name="analysis",
    )(observations, pltpu.with_memory_space_constraint(background, pltpu.VMEM))


def exchange(x):
    return lax.all_to_all(x, "member", 0, 0, tiled=True)


def per_device(ensemble, velocity, observed_column, slot_count, radius, observed_value, error_variance):
    members, height, width = ensemble.shape
    devices = lax.axis_size("tile")
    here = lax.axis_index("tile")
    up = [(i, i + 1) for i in range(devices - 1)]
    down = [(j, i) for i, j in up]
    edge = height // 8
    kept = height - 2 * edge
    groups = 2 * edge // GROUP
    inner_steps = kept // (2 * edge)

    def row_of(g):
        step, half = pl.program_id(0), groups // 2
        outer = g if g < half else height // GROUP - groups + g
        return jnp.where(step < inner_steps, half + groups * step + g, outer)

    columns = observed_column[:, 0]
    values = observed_value[:, 0]
    active = (jnp.arange(SLOTS, dtype=jnp.int32)[None, :] < slot_count).astype(jnp.float32)
    offset = (columns.astype(jnp.float32) - 0.5 * (COLS - 1)) / radius.astype(jnp.float32)
    root_weight = jnp.sqrt(active / (1.0 + offset * offset) / error_variance[:, 0])
    observations = jnp.stack([columns.astype(jnp.float32), root_weight, values])
    observations = observations.reshape(3, height // GROUP, LANE)
    edges = jnp.stack([here == 0, here == devices - 1]).astype(jnp.int32)

    above = lax.ppermute(jnp.concatenate([ensemble[:, -2:], velocity[:, -2:]], axis=0), "tile", up)
    below = lax.ppermute(jnp.concatenate([ensemble[:, :2], velocity[:, :2]], axis=0), "tile", down)
    fields = forecast_inner(ensemble, velocity, edge, kept)
    fields = forecast_edge(edges, ensemble, velocity, above, below, edge, fields)
    fields = exchange(fields.reshape(-1, height, COLS))
    done = analyse(fields, observations, groups, row_of)
    done = exchange(done)
    both = jnp.concatenate([done[:, kept : kept + edge], done[:, :kept], done[:, kept + edge :]], axis=1)
    both = both.reshape(-1, members, height, COLS)
    return both.transpose(1, 2, 0, 3).reshape(members, height, width)


def solution(mesh):
    return jax.shard_map(
        per_device,
        mesh=mesh,
        in_specs=(
            P("member", "tile", None),
            P(None, "tile", None),
            P("tile", "member", None),
            P("tile", "member"),
            P("tile", "member"),
            P("tile", "member", None),
            P("tile", "member", None),
        ),
        out_specs=P("member", "tile", None),
        check_vma=False,
    )
```

```python
import functools

import jax
import jax.numpy as jnp
from jax import lax
from jax.experimental import pallas as pl
from jax.experimental.pallas import tpu as pltpu
from jax.sharding import PartitionSpec as P

COLS = 128
SWEEPS = 6
LANE = 128
BLOCK = 2048
GROUP = 4
SLOTS = 32
SIDE = 8


def stencil(fields, wind_x, wind_y, first_col, last_col, low_row, high_row):
    rows, lanes = wind_x.shape
    face_x = 0.5 * (wind_x + pltpu.roll(wind_x, rows - 1, 0))
    before_x = pltpu.roll(face_x, 1, 0)
    face_y = 0.5 * (wind_y + pltpu.roll(wind_y, lanes - 1, 1))
    before_y = pltpu.roll(face_y, 1, 1)
    zero = jnp.zeros_like(face_x)
    centre = (
        1.0
        - jnp.maximum(face_x, 0.0)
        + jnp.minimum(before_x, 0.0)
        - jnp.maximum(face_y, 0.0)
        + jnp.minimum(before_y, 0.0)
    )
    north, south = jnp.maximum(before_x, 0.0), jnp.minimum(face_x, 0.0)
    row = lax.broadcasted_iota(jnp.int32, face_x.shape, 0)
    if low_row is not None:
        north = jnp.where(row == low_row, zero, north)
    if high_row is not None:
        south = jnp.where(row == high_row, zero, south)
    col = lax.broadcasted_iota(jnp.int32, face_x.shape, 1)
    west = jnp.where(col == first_col, zero, jnp.maximum(before_y, 0.0))
    east = jnp.where(col == last_col, zero, jnp.minimum(face_y, 0.0))

    def substep(field, part):
        return (
            centre[part] * field[part]
            + north[part] * pltpu.roll(field, 1, 0)[part]
            - south[part] * pltpu.roll(field, rows - 1, 0)[part]
            + west[part] * pltpu.roll(field, 1, 1)[part]
            - east[part] * pltpu.roll(field, lanes - 1, 1)[part]
        )

    kept = (slice(SIDE, rows - SIDE), slice(LANE, lanes - LANE))
    return [substep(substep(field, (slice(None), slice(None))), kept) for field in fields]


def advance(pieces, out_ref, out_row, low_row, high_row):
    k, last = pl.program_id(0), pl.num_programs(0) - 1
    *fields, wind_x, wind_y = pieces
    rows, lanes = wind_x.shape
    inside_left = jnp.where(k > 0, wind_y[:, :LANE], 0.0)
    inside_right = jnp.where(k < last, wind_y[:, lanes - LANE :], 0.0)
    wind_y = jnp.concatenate([inside_left, wind_y[:, LANE : lanes - LANE], inside_right], axis=1)
    first_col = jnp.where(k == 0, LANE, -1)
    last_col = jnp.where(k == last, lanes - LANE - 1, -1)
    new = stencil(fields, wind_x, wind_y, first_col, last_col, low_row, high_row)
    for m, field in enumerate(new):
        for t in range(field.shape[1] // LANE):
            out_ref[t, m, pl.ds(out_row, rows - 2 * SIDE), :] = field[:, LANE * t : LANE * (t + 1)]


def joined(refs, i, rows):
    return jnp.concatenate([ref[i, rows, :] for ref in refs], axis=1)


def inner_kernel(*refs, row0, kept):
    *refs, out_ref, up_ref, down_ref = refs
    rows = slice(row0 - SIDE, row0 + kept + SIDE)
    for i in range(4):
        middle = refs[3 * (i // 2) + 1]
        height = middle.shape[1]
        up_ref[i] = middle[i % 2, height - 2 : height, :]
        down_ref[i] = middle[i % 2, 0:2, :]
    advance([joined(refs[3 * (i // 2) : 3 * (i // 2) + 3], i % 2, rows) for i in range(4)], out_ref, 0, None, None)


def edge_kernel(edge_ref, *refs, kept):
    *refs, above_ref, below_ref, out_ref = refs
    tall, lanes = refs[0].shape[1], out_ref.shape[0] * LANE
    far = jnp.zeros((SIDE - 2, lanes + 2 * LANE), jnp.float32)
    k, width = pl.program_id(0), above_ref.shape[2]
    starts = [
        (jnp.maximum(k * lanes - LANE, 0), LANE),
        (k * lanes, lanes),
        (jnp.minimum((k + 1) * lanes, width - LANE), LANE),
    ]
    body = lambda first, i, rows: joined(refs[first + 3 * (i // 2) : first + 3 * (i // 2) + 3], i % 2, rows)
    beyond = lambda ref, i: jnp.concatenate(
        [ref[i, :, pl.ds(pl.multiple_of(start, LANE), size)] for start, size in starts], axis=1
    )
    top = [
        jnp.concatenate([far, beyond(above_ref, i), body(0, i, slice(0, kept + SIDE))], axis=0)
        for i in range(4)
    ]
    advance(top, out_ref, 0, jnp.where(edge_ref[0] == 1, SIDE, -1), None)
    bottom = [
        jnp.concatenate([body(6, i, slice(tall - kept - SIDE, tall)), beyond(below_ref, i), far], axis=0)
        for i in range(4)
    ]
    advance(bottom, out_ref, kept, None, jnp.where(edge_ref[1] == 1, SIDE + kept - 1, -1))


def vmem():
    return pl.BlockSpec(memory_space=pltpu.VMEM)


def resident(x):
    return pltpu.with_memory_space_constraint(x, pltpu.VMEM)


def around(count, height, width, row=0):
    per, last = BLOCK // LANE, width // LANE - 1
    return [
        pl.BlockSpec((count, height, LANE), lambda k: (0, row, jnp.maximum(per * k - 1, 0))),
        pl.BlockSpec((count, height, BLOCK), lambda k: (0, row, k)),
        pl.BlockSpec((count, height, LANE), lambda k: (0, row, jnp.minimum(per * (k + 1), last))),
    ]


def forecast_inner(ensemble, velocity, row0, kept):
    members, height, width = ensemble.shape
    per = BLOCK // LANE
    beyond = jax.ShapeDtypeStruct((members + 2, 2, width), jnp.float32)
    return pl.pallas_call(
        functools.partial(inner_kernel, row0=row0, kept=kept),
        grid=(width // BLOCK,),
        out_shape=[jax.ShapeDtypeStruct((width // COLS, members, kept, COLS), jnp.float32), beyond, beyond],
        in_specs=around(members, height, width) + around(2, height, width),
        out_specs=[pl.BlockSpec((per, members, kept, COLS), lambda k: (k, 0, 0, 0))]
        + [pl.BlockSpec((members + 2, 2, BLOCK), lambda k: (0, 0, k))] * 2,
        name="forecast_inner",
    )(*[ensemble] * 3, *[velocity] * 3)


def forecast_edge(edges, ensemble, velocity, above, below, kept):
    members, height, width = ensemble.shape
    per = BLOCK // LANE
    tall = kept + SIDE
    both = lambda row: around(members, tall, width, row) + around(2, tall, width, row)
    return pl.pallas_call(
        functools.partial(edge_kernel, kept=kept),
        grid=(width // BLOCK,),
        out_shape=jax.ShapeDtypeStruct((width // COLS, members, 2 * kept, COLS), jnp.float32),
        in_specs=[pl.BlockSpec(memory_space=pltpu.SMEM)]
        + both(0)
        + both(height // tall - 1)
        + [vmem(), vmem()],
        out_specs=pl.BlockSpec((per, members, 2 * kept, COLS), lambda k: (k, 0, 0, 0)),
        name="forecast_edge",
        compiler_params=pltpu.CompilerParams(vmem_limit_bytes=48 << 20),
    )(edges, *([ensemble] * 3 + [velocity] * 3) * 2, resident(above), resident(below))


def split(x, parts=2):
    out = []
    for _ in range(parts - 1):
        out.append(x.astype(jnp.bfloat16))
        x = x - out[-1].astype(jnp.float32)
    return [*out, x.astype(jnp.bfloat16)]


def mm(a, b, dim=0):
    return lax.dot_general(a, b, (((1,), (dim,)), ((), ())), preferred_element_type=jnp.float32)


def product(left, right, dim=0):
    rows = left[0].shape[0]
    total = None
    for i in reversed(range(len(right))):
        kept = left[: len(right) - i]
        both = mm(jnp.concatenate(kept, axis=0), right[i], dim)
        for j in reversed(range(len(kept))):
            part = both[rows * j : rows * (j + 1)]
            total = part if total is None else total + part
    return total


def times(left, right):
    return product(split(left, len(right)), right)


def tile_of(ref, tile):
    members, tiles, width = ref.shape
    return ref.reshape(members * tiles, width).at[pl.ds(tile, members, stride=tiles), :]


def analysis_kernel(obs_ref, x_ref, out_ref, *, groups, first, row_of):
    members = x_ref.shape[0]
    spare = members - 1.0
    wide = GROUP * members
    lane = lax.broadcasted_iota(jnp.int32, (1, LANE), 1)
    slots_of = [(lane // SLOTS) == b for b in range(GROUP)]

    def indicator(shape, row_size, col_size):
        row = lax.broadcasted_iota(jnp.int32, shape, 0) // row_size
        col = lax.broadcasted_iota(jnp.int32, shape, 1) // col_size
        return jnp.where(row == col, 1.0, 0.0).astype(jnp.bfloat16)

    block = indicator((wide, wide), members, members)
    slot_block = indicator((wide, LANE), members, SLOTS)
    eye = jnp.where(
        lax.broadcasted_iota(jnp.int32, (members, wide), 0)
        == lax.broadcasted_iota(jnp.int32, (members, wide), 1) % members,
        1.0,
        0.0,
    )
    spare_rows = jnp.zeros((15, wide), jnp.float32)
    per = LANE // members
    first_half = lax.broadcasted_iota(jnp.int32, (members, LANE), 1) < members
    first_half16 = jnp.where(first_half, 1.0, 0.0).astype(jnp.bfloat16)
    base = pl.program_id(0) * (groups * GROUP)

    def stacked(parts, mask):
        return [jnp.concatenate([part] * GROUP, axis=0) * mask for part in parts]

    def one(g):
        averages, anomalies = [], []
        spread = jnp.zeros((members, LANE), jnp.float32)
        there = jnp.zeros((8, LANE), jnp.float32)
        row = pl.ds(row_of(g), 1)
        index = jnp.broadcast_to(obs_ref[0, row, :].astype(jnp.int32), (members, LANE))
        for b in range(GROUP):
            x = tile_of(x_ref, base + g * GROUP + b)[...]
            average = jnp.mean(x, axis=0, keepdims=True)
            anomaly = x - average
            averages.append(average)
            anomalies.append(anomaly)
            seen = jnp.take_along_axis(anomaly, index, axis=1, mode="promise_in_bounds")
            spread = jnp.where(slots_of[b], seen, spread)
            mean_seen = jnp.take_along_axis(
                jnp.broadcast_to(average, (8, LANE)), index[:8], axis=1, mode="promise_in_bounds"
            )
            there = jnp.where(slots_of[b], mean_seen, there)
        root = obs_ref[1, row, :]
        scaled = spread * root
        innovation = root * (obs_ref[2, row, :] - there[:1])
        yield
        scaled_split = split(scaled)
        wanted = jnp.concatenate([innovation, spare_rows[:, :LANE]], axis=0)
        left = [jnp.concatenate(pair, axis=0) for pair in zip(scaled_split, split(wanted))]
        stage = product(left, stacked(scaled_split, slot_block), 1)
        system = stage[:members] + spare * eye
        wanted = stage[members:]
        yield
        squares = jnp.sum(system * system, axis=0, keepdims=True)
        pieces = split(squares, 3) + [jnp.zeros((13, wide), jnp.bfloat16)]
        total = jnp.sum(mm(jnp.concatenate(pieces, axis=0), block), axis=0, keepdims=True)
        yield
        inverse = 1.0 / jnp.sqrt(total)
        root_norm = jnp.sqrt(inverse)
        system = system * inverse
        result = None
        for number in range(SWEEPS):
            factor = 1.5 * eye - 0.5 * system
            right = stacked(split(factor), block)
            last = number == SWEEPS - 1
            if last:
                result = times(result, right)
            elif number == 0:
                stage, result = times(system, right), factor
            else:
                stage = times(jnp.concatenate([system, result], axis=0), right)
                result = stage[members:]
            yield
            if not last:
                system = times(stage[:members], right)
                yield
        right = stacked(split(result), block)
        wanted = times(wanted, right)
        yield
        mean_weight = times(wanted, right)[:1] * inverse
        yield
        high, low = split((spare**0.5 * root_norm) * result + mean_weight)
        for b in range(GROUP):
            at = LANE * (b // per)
            here, there_low = high[:, at : at + LANE], low[:, at : at + LANE]
            turned = lambda part: pltpu.roll(part.astype(jnp.float32), members, 1).astype(jnp.bfloat16)
            if b % per:
                left = jnp.where(first_half, turned(here), there_low)
            else:
                left = jnp.where(first_half, here, turned(there_low))
            left = jnp.concatenate([left, left * first_half16], axis=1)
            a_high, a_low = split(anomalies[b])
            right = jnp.concatenate([a_high, a_high, a_low, jnp.zeros_like(a_low)], axis=0)
            tile_of(out_ref, first + base + g * GROUP + b)[...] = mm(left, right) + averages[b]
        yield

    running = [one(g) for g in range(groups)]
    while running:
        running = [r for r in running if next(r, running) is None]


def analyse(background, observations, groups, total, first, row_of, earlier=None):
    members, rows, width = background.shape
    kernel = functools.partial(analysis_kernel, groups=groups, first=first, row_of=row_of)
    more = {}
    if earlier is not None:
        plain = kernel
        kernel = lambda o, x, _, out: plain(o, x, out)
        more = {"input_output_aliases": {2: 0}}
    return pl.pallas_call(
        kernel,
        grid=(rows // (groups * GROUP),),
        out_shape=pltpu.VMEM((members, total, width), jnp.float32),
        in_specs=[vmem()] * (2 + len(more)),
        out_specs=vmem(),
        compiler_params=pltpu.CompilerParams(vmem_limit_bytes=32 << 20),
        name="analysis",
        **more,
    )(observations, resident(background), *([] if earlier is None else [resident(earlier)]))


def exchange(x):
    return lax.all_to_all(x, "member", 0, 0, tiled=True)


def per_device(ensemble, velocity, observed_column, slot_count, radius, observed_value, error_variance):
    members, height, width = ensemble.shape
    devices = lax.axis_size("tile")
    here = lax.axis_index("tile")
    up = [(i, i + 1) for i in range(devices - 1)]
    down = [(j, i) for i, j in up]
    edge = height // 8
    kept = height - 2 * edge
    groups = 2 * edge // GROUP
    half = groups // 2
    inner_row = lambda g: half + groups * pl.program_id(0) + g
    outer_row = lambda g: g if g < half else height // GROUP - groups + g

    columns = observed_column[:, 0]
    values = observed_value[:, 0]
    active = (jnp.arange(SLOTS, dtype=jnp.int32)[None, :] < slot_count).astype(jnp.float32)
    offset = (columns.astype(jnp.float32) - 0.5 * (COLS - 1)) / radius.astype(jnp.float32)
    root_weight = jnp.sqrt(active / (1.0 + offset * offset) / error_variance[:, 0])
    observations = jnp.stack([columns.astype(jnp.float32), root_weight, values])
    observations = observations.reshape(3, height // GROUP, LANE)
    edges = jnp.stack([here == 0, here == devices - 1]).astype(jnp.int32)

    first, to_next, to_last = forecast_inner(ensemble, velocity, edge, kept)
    above = lax.ppermute(to_next, "tile", up)
    below = lax.ppermute(to_last, "tile", down)
    first = exchange(first.reshape(-1, kept, COLS))
    second = forecast_edge(edges, ensemble, velocity, above, below, edge)
    second = exchange(second.reshape(-1, 2 * edge, COLS))
    done = analyse(first, observations, groups, height, 0, inner_row)
    done = analyse(second, observations, groups, height, kept, outer_row, done)
    done = exchange(done)
    both = jnp.concatenate([done[:, kept : kept + edge], done[:, :kept], done[:, kept + edge :]], axis=1)
    both = both.reshape(-1, members, height, COLS)
    return both.transpose(1, 2, 0, 3).reshape(members, height, width)


def solution(mesh):
    return jax.shard_map(
        per_device,
        mesh=mesh,
        in_specs=(
            P("member", "tile", None),
            P(None, "tile", None),
            P("tile", "member", None),
            P("tile", "member"),
            P("tile", "member"),
            P("tile", "member", None),
            P("tile", "member", None),
        ),
        out_specs=P("member", "tile", None),
        check_vma=False,
    )
```

```python
import functools

import jax
import jax.numpy as jnp
from jax import lax
from jax.experimental import pallas as pl
from jax.experimental.pallas import tpu as pltpu
from jax.sharding import Mesh
from jax.sharding import PartitionSpec as P

CHIP = ("member_z", "member_y")
CORE = "member_core"
MEMBER = (*CHIP, CORE)
COLS = 128
SWEEPS = 6
LANE = 128
BLOCK = 2048
GROUP = 4
SLOTS = 32
SIDE = 8


def stencil(fields, wind_x, wind_y, first_col, last_col, low_row, high_row):
    rows, lanes = wind_x.shape
    face_x = 0.5 * (wind_x + pltpu.roll(wind_x, rows - 1, 0))
    before_x = pltpu.roll(face_x, 1, 0)
    face_y = 0.5 * (wind_y + pltpu.roll(wind_y, lanes - 1, 1))
    before_y = pltpu.roll(face_y, 1, 1)
    zero = jnp.zeros_like(face_x)
    centre = (
        1.0
        - jnp.maximum(face_x, 0.0)
        + jnp.minimum(before_x, 0.0)
        - jnp.maximum(face_y, 0.0)
        + jnp.minimum(before_y, 0.0)
    )
    north, south = jnp.maximum(before_x, 0.0), jnp.minimum(face_x, 0.0)
    row = lax.broadcasted_iota(jnp.int32, face_x.shape, 0)
    if low_row is not None:
        north = jnp.where(row == low_row, zero, north)
    if high_row is not None:
        south = jnp.where(row == high_row, zero, south)
    col = lax.broadcasted_iota(jnp.int32, face_x.shape, 1)
    west = jnp.where(col == first_col, zero, jnp.maximum(before_y, 0.0))
    east = jnp.where(col == last_col, zero, jnp.minimum(face_y, 0.0))

    def substep(field, part):
        return (
            centre[part] * field[part]
            + north[part] * pltpu.roll(field, 1, 0)[part]
            - south[part] * pltpu.roll(field, rows - 1, 0)[part]
            + west[part] * pltpu.roll(field, 1, 1)[part]
            - east[part] * pltpu.roll(field, lanes - 1, 1)[part]
        )

    kept = (slice(SIDE, rows - SIDE), slice(LANE, lanes - LANE))
    return [substep(substep(field, (slice(None), slice(None))), kept) for field in fields]


def advance(pieces, store, low_row, high_row):
    k, last = pl.program_id(0), pl.num_programs(0) - 1
    *fields, wind_x, wind_y = pieces
    _, lanes = wind_x.shape
    inside_left = jnp.where(k > 0, wind_y[:, :LANE], 0.0)
    inside_right = jnp.where(k < last, wind_y[:, lanes - LANE :], 0.0)
    wind_y = jnp.concatenate([inside_left, wind_y[:, LANE : lanes - LANE], inside_right], axis=1)
    first_col = jnp.where(k == 0, LANE, -1)
    last_col = jnp.where(k == last, lanes - LANE - 1, -1)
    new = stencil(fields, wind_x, wind_y, first_col, last_col, low_row, high_row)
    count = lanes // LANE - 2
    for m, field in enumerate(new):
        for t in range(count):
            store(k * count, t, m, field[:, LANE * t : LANE * (t + 1)])


def joined(refs, i, rows):
    return jnp.concatenate([ref[i, rows, :] for ref in refs], axis=1)


def inner_kernel(edge_ref, *refs, row0, kept):
    *refs, out_ref, near_ref, far_ref = refs
    odd = edge_ref[2] == 1
    rows = slice(row0 - SIDE, row0 + kept + SIDE)
    for i in range(4):
        middle = refs[3 * (i // 2) + 1]
        height = middle.shape[1]
        span = pl.ds(pl.multiple_of(pl.program_id(0) * middle.shape[2], LANE), middle.shape[2])
        first, last = middle[i % 2, 0:2, :], middle[i % 2, height - 2 : height, :]
        near_ref[i, :, span] = jnp.where(odd, first, last)
        far_ref[i, :, span] = jnp.where(odd, last, first)

    def store(base, t, m, field):
        out_ref[base + t, m] = field

    advance([joined(refs[3 * (i // 2) : 3 * (i // 2) + 3], i % 2, rows) for i in range(4)], store, None, None)


def edge_kernel(edge_ref, *refs, kept):
    *refs, near_ref, far_ref, out_ref = refs
    odd = edge_ref[2] == 1
    tall, lanes = refs[0].shape[1], refs[1].shape[2]
    far = jnp.zeros((SIDE - 2, lanes + 2 * LANE), jnp.float32)
    k, width = pl.program_id(0), near_ref.shape[2]
    starts = [
        (jnp.maximum(k * lanes - LANE, 0), LANE),
        (k * lanes, lanes),
        (jnp.minimum((k + 1) * lanes, width - LANE), LANE),
    ]
    body = lambda first, i, rows: joined(refs[first + 3 * (i // 2) : first + 3 * (i // 2) + 3], i % 2, rows)
    spans = [pl.ds(pl.multiple_of(start, LANE), size) for start, size in starts]
    of = lambda ref, i: jnp.concatenate([ref[i, :, span] for span in spans], axis=1)
    beyond = lambda above, i: jnp.where(odd == above, of(near_ref, i), of(far_ref, i))
    top = [
        jnp.concatenate([far, beyond(True, i), body(0, i, slice(0, kept + SIDE))], axis=0)
        for i in range(4)
    ]

    def store_at(row):
        def store(base, t, m, field):
            out_ref[(t % 2) ^ edge_ref[3], base // 2 + t // 2, m, pl.ds(row, kept), :] = field

        return store

    advance(top, store_at(0), jnp.where(edge_ref[0] == 1, SIDE, -1), None)
    bottom = [
        jnp.concatenate([body(6, i, slice(tall - kept - SIDE, tall)), beyond(False, i), far], axis=0)
        for i in range(4)
    ]
    advance(bottom, store_at(kept), None, jnp.where(edge_ref[1] == 1, SIDE + kept - 1, -1))


def vmem():
    return pl.BlockSpec(memory_space=pltpu.VMEM)


def resident(x):
    return pltpu.with_memory_space_constraint(x, pltpu.VMEM)


def around(count, height, width, row=0):
    per, last = BLOCK // LANE, width // LANE - 1
    return [
        pl.BlockSpec((count, height, LANE), lambda k: (0, row, jnp.maximum(per * k - 1, 0))),
        pl.BlockSpec((count, height, BLOCK), lambda k: (0, row, k)),
        pl.BlockSpec((count, height, LANE), lambda k: (0, row, jnp.minimum(per * (k + 1), last))),
    ]


def forecast_inner(edges, ensemble, velocity, row0, kept):
    members, height, width = ensemble.shape
    beyond = pltpu.VMEM((members + 2, 2, width), jnp.float32)
    return pl.pallas_call(
        functools.partial(inner_kernel, row0=row0, kept=kept),
        grid=(width // BLOCK,),
        out_shape=[pltpu.VMEM((width // COLS, members, kept, COLS), jnp.float32), beyond, beyond],
        in_specs=[pl.BlockSpec(memory_space=pltpu.SMEM)] + around(members, height, width) + around(2, height, width),
        out_specs=[vmem()] * 3,
        name="forecast_inner",
        compiler_params=pltpu.CompilerParams(vmem_limit_bytes=24 << 20),
    )(edges, *[ensemble] * 3, *[velocity] * 3)


def forecast_edge(edges, ensemble, velocity, near, far, kept):
    members, height, width = ensemble.shape
    tall = kept + SIDE
    both = lambda row: around(members, tall, width, row) + around(2, tall, width, row)
    return pl.pallas_call(
        functools.partial(edge_kernel, kept=kept),
        grid=(width // BLOCK,),
        out_shape=pltpu.VMEM((2, width // COLS // 2, members, 2 * kept, COLS), jnp.float32),
        in_specs=[pl.BlockSpec(memory_space=pltpu.SMEM)]
        + both(0)
        + both(height // tall - 1)
        + [vmem(), vmem()],
        out_specs=vmem(),
        name="forecast_edge",
        compiler_params=pltpu.CompilerParams(vmem_limit_bytes=24 << 20),
    )(edges, *([ensemble] * 3 + [velocity] * 3) * 2, resident(near), resident(far))


def split(x, parts=2):
    out = []
    for _ in range(parts - 1):
        out.append(x.astype(jnp.bfloat16))
        x = x - out[-1].astype(jnp.float32)
    return [*out, x.astype(jnp.bfloat16)]


def mm(a, b, dim=0):
    return lax.dot_general(a, b, (((1,), (dim,)), ((), ())), preferred_element_type=jnp.float32)


def product(left, right, dim=0):
    rows = left[0].shape[0]
    total = None
    for i in reversed(range(len(right))):
        kept = left[: len(right) - i]
        both = mm(jnp.concatenate(kept, axis=0), right[i], dim)
        for j in reversed(range(len(kept))):
            part = both[rows * j : rows * (j + 1)]
            total = part if total is None else total + part
    return total


def times(left, right):
    return product(split(left, len(right)), right)


def tile_of(ref, tile):
    members, tiles, width = ref.shape
    return ref.reshape(members * tiles, width).at[pl.ds(tile, members, stride=tiles), :]


def analysis_kernel(obs_ref, x_ref, out_ref, *, groups, first, row_of, blocked=False):
    members = x_ref.shape[0]
    spare = members - 1.0
    wide = GROUP * members
    lane = lax.broadcasted_iota(jnp.int32, (1, LANE), 1)
    slots_of = [(lane // SLOTS) == b for b in range(GROUP)]

    def indicator(shape, row_size, col_size):
        row = lax.broadcasted_iota(jnp.int32, shape, 0) // row_size
        col = lax.broadcasted_iota(jnp.int32, shape, 1) // col_size
        return jnp.where(row == col, 1.0, 0.0).astype(jnp.bfloat16)

    block = indicator((wide, wide), members, members)
    slot_block = indicator((wide, LANE), members, SLOTS)
    eye = jnp.where(
        lax.broadcasted_iota(jnp.int32, (members, wide), 0)
        == lax.broadcasted_iota(jnp.int32, (members, wide), 1) % members,
        1.0,
        0.0,
    )
    spare_rows = jnp.zeros((15, wide), jnp.float32)
    per = LANE // members
    first_half = lax.broadcasted_iota(jnp.int32, (members, LANE), 1) < members
    first_half16 = jnp.where(first_half, 1.0, 0.0).astype(jnp.bfloat16)
    base = pl.program_id(0) * (groups * GROUP)

    def stacked(parts, mask):
        return [jnp.concatenate([part] * GROUP, axis=0) * mask for part in parts]

    def one(g):
        averages, anomalies = [], []
        spread = jnp.zeros((members, LANE), jnp.float32)
        there = jnp.zeros((8, LANE), jnp.float32)
        row = pl.ds(row_of(g), 1)
        index = jnp.broadcast_to(obs_ref[0, row, :].astype(jnp.int32), (members, LANE))
        for b in range(GROUP):
            x = tile_of(x_ref, (0 if blocked else base) + g * GROUP + b)[...]
            average = jnp.mean(x, axis=0, keepdims=True)
            anomaly = x - average
            averages.append(average)
            anomalies.append(anomaly)
            seen = jnp.take_along_axis(anomaly, index, axis=1, mode="promise_in_bounds")
            spread = jnp.where(slots_of[b], seen, spread)
            mean_seen = jnp.take_along_axis(
                jnp.broadcast_to(average, (8, LANE)), index[:8], axis=1, mode="promise_in_bounds"
            )
            there = jnp.where(slots_of[b], mean_seen, there)
        root = obs_ref[1, row, :]
        scaled = spread * root
        innovation = root * (obs_ref[2, row, :] - there[:1])
        yield
        scaled_split = split(scaled)
        wanted = jnp.concatenate([innovation, spare_rows[:, :LANE]], axis=0)
        left = [jnp.concatenate(pair, axis=0) for pair in zip(scaled_split, split(wanted))]
        stage = product(left, stacked(scaled_split, slot_block), 1)
        system = stage[:members] + spare * eye
        wanted = stage[members:]
        yield
        squares = jnp.sum(system * system, axis=0, keepdims=True)
        pieces = split(squares, 3) + [jnp.zeros((13, wide), jnp.bfloat16)]
        total = jnp.sum(mm(jnp.concatenate(pieces, axis=0), block), axis=0, keepdims=True)
        yield
        inverse = 1.0 / jnp.sqrt(total)
        root_norm = jnp.sqrt(inverse)
        system = system * inverse
        result = None
        for number in range(SWEEPS):
            factor = 1.5 * eye - 0.5 * system
            right = stacked(split(factor), block)
            last = number == SWEEPS - 1
            if last:
                result = times(result, right)
            elif number == 0:
                stage, result = times(system, right), factor
            else:
                stage = times(jnp.concatenate([system, result], axis=0), right)
                result = stage[members:]
            yield
            if not last:
                system = times(stage[:members], right)
                yield
        right = stacked(split(result), block)
        wanted = times(wanted, right)
        yield
        mean_weight = times(wanted, right)[:1] * inverse
        yield
        high, low = split((spare**0.5 * root_norm) * result + mean_weight)
        for b in range(GROUP):
            at = LANE * (b // per)
            here, there_low = high[:, at : at + LANE], low[:, at : at + LANE]
            turned = lambda part: pltpu.roll(part.astype(jnp.float32), members, 1).astype(jnp.bfloat16)
            if b % per:
                left = jnp.where(first_half, turned(here), there_low)
            else:
                left = jnp.where(first_half, here, turned(there_low))
            left = jnp.concatenate([left, left * first_half16], axis=1)
            a_high, a_low = split(anomalies[b])
            right = jnp.concatenate([a_high, a_high, a_low, jnp.zeros_like(a_low)], axis=0)
            tile_of(out_ref, first + base + g * GROUP + b)[...] = mm(left, right) + averages[b]
        yield

    running = [one(g) for g in range(groups)]
    while running:
        running = [r for r in running if next(r, running) is None]


def analyse(background, observations, groups, total, first, row_of, earlier=None):
    members, rows, width = background.shape
    tiles = groups * GROUP
    kernel = functools.partial(analysis_kernel, groups=groups, first=first, row_of=row_of)
    call = functools.partial(
        pl.pallas_call,
        grid=(rows // tiles,),
        out_shape=pltpu.VMEM((members, total, width), jnp.float32),
        out_specs=vmem(),
        compiler_params=pltpu.CompilerParams(vmem_limit_bytes=32 << 20),
        name="analysis",
    )
    if earlier is None:
        field = pl.BlockSpec((members, tiles, width), lambda i: (0, i, 0))
        background = pltpu.with_memory_space_constraint(background, pltpu.HBM)
        return call(functools.partial(kernel, blocked=True), in_specs=[vmem(), field])(observations, background)
    return call(
        lambda o, x, _, out: kernel(o, x, out),
        in_specs=[vmem()] * 3,
        input_output_aliases={2: 0},
    )(observations, resident(background), resident(earlier))


def exchange(x, axes=MEMBER):
    return lax.all_to_all(x, axes, 0, 0, tiled=True)


def per_device(ensemble, velocity, observed_column, slot_count, radius, observed_value, error_variance):
    members, height, width = ensemble.shape
    ensemble, velocity = (pltpu.with_memory_space_constraint(a, pltpu.HBM) for a in (ensemble, velocity))
    devices = lax.axis_size("tile")
    here = lax.axis_index("tile")
    edge = height // 8
    kept = height - 2 * edge
    groups = 2 * edge // GROUP
    half = groups // 2
    inner_row = lambda g: half + groups * pl.program_id(0) + g
    outer_row = lambda g: g if g < half else height // GROUP - groups + g

    columns = observed_column[:, 0]
    values = observed_value[:, 0]
    active = (jnp.arange(SLOTS, dtype=jnp.int32)[None, :] < slot_count).astype(jnp.float32)
    offset = (columns.astype(jnp.float32) - 0.5 * (COLS - 1)) / radius.astype(jnp.float32)
    root_weight = jnp.sqrt(active / (1.0 + offset * offset) / error_variance[:, 0])
    observations = jnp.stack([columns.astype(jnp.float32), root_weight, values])
    observations = observations.reshape(3, height // GROUP, LANE)

    core = lax.axis_index(CORE)
    edges = jnp.stack([here == 0, here == devices - 1, here % 2 == 1, core == 1]).astype(jnp.int32)
    first, to_near, to_far = forecast_inner(edges, ensemble, velocity, edge, kept)
    near = lax.ppermute(to_near, "tile", [(i, i ^ 1) for i in range(devices)])
    first = exchange(first.reshape(-1, kept, COLS))
    inside = range(1, devices - 1)
    far = lax.ppermute(to_far, "tile", [(i, i + 1 if i % 2 else i - 1) for i in inside])
    second = forecast_edge(edges, ensemble, velocity, near, far, edge)
    mine, swapped = second[0], lax.ppermute(second[1], CORE, [(0, 1), (1, 0)])
    second = jnp.where(core == 0, jnp.stack([mine, swapped], axis=1), jnp.stack([swapped, mine], axis=1))
    second = exchange(second.reshape(-1, 2 * edge, COLS), CHIP)
    done = analyse(first, observations, groups, height, 0, inner_row)
    done = analyse(second, observations, groups, height, kept, outer_row, done)
    done = exchange(done)
    both = jnp.concatenate([done[:, kept : kept + edge], done[:, :kept], done[:, kept + edge :]], axis=1)
    both = both.reshape(-1, members, height, COLS)
    return both.transpose(1, 2, 0, 3).reshape(members, height, width)


def solution(mesh):
    torus = Mesh(mesh.devices.reshape(4, 4, 2, mesh.shape["tile"]), (*MEMBER, "tile"))
    return jax.shard_map(
        per_device,
        mesh=torus,
        in_specs=(
            P(MEMBER, "tile", None),
            P(None, "tile", None),
            P("tile", MEMBER, None),
            P("tile", MEMBER),
            P("tile", MEMBER),
            P("tile", MEMBER, None),
            P("tile", MEMBER, None),
        ),
        out_specs=P(MEMBER, "tile", None),
        check_vma=False,
    )
```

```python
import functools

import jax
import jax.numpy as jnp
from jax import lax
from jax.experimental import pallas as pl
from jax.experimental.pallas import tpu as pltpu
from jax.sharding import Mesh
from jax.sharding import PartitionSpec as P

CHIP = ("member_z", "member_y")
CORE = "member_core"
MEMBER = (*CHIP, CORE)
COLS = 128
SWEEPS = 6
LANE = 128
BLOCK = 2048
GROUP = 4
SLOTS = 32
SIDE = 8


def stencil(fields, wind_x, wind_y, first_col, last_col, low_row, high_row):
    rows, lanes = wind_x.shape
    face_x = 0.5 * (wind_x + pltpu.roll(wind_x, rows - 1, 0))
    before_x = pltpu.roll(face_x, 1, 0)
    face_y = 0.5 * (wind_y + pltpu.roll(wind_y, lanes - 1, 1))
    before_y = pltpu.roll(face_y, 1, 1)
    zero = jnp.zeros_like(face_x)
    centre = (
        1.0
        - jnp.maximum(face_x, 0.0)
        + jnp.minimum(before_x, 0.0)
        - jnp.maximum(face_y, 0.0)
        + jnp.minimum(before_y, 0.0)
    )
    north, south = jnp.maximum(before_x, 0.0), jnp.minimum(face_x, 0.0)
    row = lax.broadcasted_iota(jnp.int32, face_x.shape, 0)
    if low_row is not None:
        north = jnp.where(row == low_row, zero, north)
    if high_row is not None:
        south = jnp.where(row == high_row, zero, south)
    col = lax.broadcasted_iota(jnp.int32, face_x.shape, 1)
    west = jnp.where(col == first_col, zero, jnp.maximum(before_y, 0.0))
    east = jnp.where(col == last_col, zero, jnp.minimum(face_y, 0.0))

    def substep(field, part):
        return (
            centre[part] * field[part]
            + north[part] * pltpu.roll(field, 1, 0)[part]
            - south[part] * pltpu.roll(field, rows - 1, 0)[part]
            + west[part] * pltpu.roll(field, 1, 1)[part]
            - east[part] * pltpu.roll(field, lanes - 1, 1)[part]
        )

    kept = (slice(SIDE, rows - SIDE), slice(LANE, lanes - LANE))
    return [substep(substep(field, (slice(None), slice(None))), kept) for field in fields]


def advance(pieces, store, low_row, high_row):
    k, last = pl.program_id(0), pl.num_programs(0) - 1
    *fields, wind_x, wind_y = pieces
    _, lanes = wind_x.shape
    inside_left = jnp.where(k > 0, wind_y[:, :LANE], 0.0)
    inside_right = jnp.where(k < last, wind_y[:, lanes - LANE :], 0.0)
    wind_y = jnp.concatenate([inside_left, wind_y[:, LANE : lanes - LANE], inside_right], axis=1)
    first_col = jnp.where(k == 0, LANE, -1)
    last_col = jnp.where(k == last, lanes - LANE - 1, -1)
    new = stencil(fields, wind_x, wind_y, first_col, last_col, low_row, high_row)
    count = lanes // LANE - 2
    for m, field in enumerate(new):
        for t in range(count):
            store(k * count, t, m, field[:, LANE * t : LANE * (t + 1)])


def joined(refs, i, rows):
    return jnp.concatenate([ref[i, rows, :] for ref in refs], axis=1)


def inner_kernel(edge_ref, *refs, row0, kept):
    *refs, out_ref, near_ref, far_ref = refs
    odd = edge_ref[2] == 1
    rows = slice(row0 - SIDE, row0 + kept + SIDE)
    for i in range(4):
        middle = refs[3 * (i // 2) + 1]
        height = middle.shape[1]
        span = pl.ds(pl.multiple_of(pl.program_id(0) * middle.shape[2], LANE), middle.shape[2])
        first, last = middle[i % 2, 0:2, :], middle[i % 2, height - 2 : height, :]
        near_ref[i, :, span] = jnp.where(odd, first, last)
        far_ref[i, :, span] = jnp.where(odd, last, first)

    def store(base, t, m, field):
        out_ref[base + t, m] = field

    advance([joined(refs[3 * (i // 2) : 3 * (i // 2) + 3], i % 2, rows) for i in range(4)], store, None, None)


def edge_kernel(edge_ref, *refs, kept):
    *refs, near_ref, far_ref, out_ref = refs
    odd = edge_ref[2] == 1
    tall, lanes = refs[0].shape[1], refs[1].shape[2]
    far = jnp.zeros((SIDE - 2, lanes + 2 * LANE), jnp.float32)
    k, width = pl.program_id(0), near_ref.shape[2]
    starts = [
        (jnp.maximum(k * lanes - LANE, 0), LANE),
        (k * lanes, lanes),
        (jnp.minimum((k + 1) * lanes, width - LANE), LANE),
    ]
    body = lambda first, i, rows: joined(refs[first + 3 * (i // 2) : first + 3 * (i // 2) + 3], i % 2, rows)
    spans = [pl.ds(pl.multiple_of(start, LANE), size) for start, size in starts]
    of = lambda ref, i: jnp.concatenate([ref[i, :, span] for span in spans], axis=1)
    beyond = lambda above, i: jnp.where(odd == above, of(near_ref, i), of(far_ref, i))
    top = [
        jnp.concatenate([far, beyond(True, i), body(0, i, slice(0, kept + SIDE))], axis=0)
        for i in range(4)
    ]

    def store_at(row):
        def store(base, t, m, field):
            out_ref[(t % 2) ^ edge_ref[3], base // 2 + t // 2, m, pl.ds(row, kept), :] = field

        return store

    advance(top, store_at(0), jnp.where(edge_ref[0] == 1, SIDE, -1), None)
    bottom = [
        jnp.concatenate([body(6, i, slice(tall - kept - SIDE, tall)), beyond(False, i), far], axis=0)
        for i in range(4)
    ]
    advance(bottom, store_at(kept), None, jnp.where(edge_ref[1] == 1, SIDE + kept - 1, -1))


def vmem():
    return pl.BlockSpec(memory_space=pltpu.VMEM)


def resident(x):
    return pltpu.with_memory_space_constraint(x, pltpu.VMEM)


def around(count, height, width, row=0):
    per, last = BLOCK // LANE, width // LANE - 1
    return [
        pl.BlockSpec((count, height, LANE), lambda k: (0, row, jnp.maximum(per * k - 1, 0))),
        pl.BlockSpec((count, height, BLOCK), lambda k: (0, row, k)),
        pl.BlockSpec((count, height, LANE), lambda k: (0, row, jnp.minimum(per * (k + 1), last))),
    ]


def forecast_inner(edges, ensemble, velocity, row0, kept):
    members, height, width = ensemble.shape
    beyond = pltpu.VMEM((members + 2, 2, width), jnp.float32)
    return pl.pallas_call(
        functools.partial(inner_kernel, row0=row0, kept=kept),
        grid=(width // BLOCK,),
        out_shape=[pltpu.VMEM((width // COLS, members, kept, COLS), jnp.float32), beyond, beyond],
        in_specs=[pl.BlockSpec(memory_space=pltpu.SMEM)] + around(members, height, width) + around(2, height, width),
        out_specs=[vmem()] * 3,
        name="forecast_inner",
        compiler_params=pltpu.CompilerParams(vmem_limit_bytes=24 << 20),
    )(edges, *[ensemble] * 3, *[velocity] * 3)


def forecast_edge(edges, ensemble, velocity, near, far, kept):
    members, height, width = ensemble.shape
    tall = kept + SIDE
    both = lambda row: around(members, tall, width, row) + around(2, tall, width, row)
    return pl.pallas_call(
        functools.partial(edge_kernel, kept=kept),
        grid=(width // BLOCK,),
        out_shape=pltpu.VMEM((2, width // COLS // 2, members, 2 * kept, COLS), jnp.float32),
        in_specs=[pl.BlockSpec(memory_space=pltpu.SMEM)]
        + both(0)
        + both(height // tall - 1)
        + [vmem(), vmem()],
        out_specs=vmem(),
        name="forecast_edge",
        compiler_params=pltpu.CompilerParams(vmem_limit_bytes=24 << 20),
    )(edges, *([ensemble] * 3 + [velocity] * 3) * 2, resident(near), resident(far))


def merge_kernel(edge_ref, both_ref, swapped_ref, out_ref):
    core = edge_ref[3]
    out_ref[:, core] = both_ref[0]
    out_ref[:, 1 - core] = swapped_ref[...]


def merge(edges, both, swapped):
    chips, *rest = swapped.shape
    return pl.pallas_call(
        merge_kernel,
        out_shape=pltpu.VMEM((chips, 2, *rest), jnp.float32),
        in_specs=[pl.BlockSpec(memory_space=pltpu.SMEM), vmem(), vmem()],
        out_specs=vmem(),
        compiler_params=pltpu.CompilerParams(vmem_limit_bytes=125 << 19),
        name="merge",
    )(edges, resident(both), resident(swapped))


def split(x, parts=2):
    out = []
    for _ in range(parts - 1):
        out.append(x.astype(jnp.bfloat16))
        x = x - out[-1].astype(jnp.float32)
    return [*out, x.astype(jnp.bfloat16)]


def mm(a, b, dim=0):
    return lax.dot_general(a, b, (((1,), (dim,)), ((), ())), preferred_element_type=jnp.float32)


def product(left, right, dim=0):
    rows = left[0].shape[0]
    total = None
    for i in reversed(range(len(right))):
        kept = left[: len(right) - i]
        both = mm(jnp.concatenate(kept, axis=0), right[i], dim)
        for j in reversed(range(len(kept))):
            part = both[rows * j : rows * (j + 1)]
            total = part if total is None else total + part
    return total


def times(left, right):
    return product(split(left, len(right)), right)


def tile_of(ref, tile):
    members, tiles, width = ref.shape
    return ref.reshape(members * tiles, width).at[pl.ds(tile, members, stride=tiles), :]


def analysis_kernel(obs_ref, x_ref, out_ref, *, groups, first, row_of, blocked=False):
    members = x_ref.shape[0]
    spare = members - 1.0
    wide = GROUP * members
    lane = lax.broadcasted_iota(jnp.int32, (1, LANE), 1)
    slots_of = [(lane // SLOTS) == b for b in range(GROUP)]

    def indicator(shape, row_size, col_size):
        row = lax.broadcasted_iota(jnp.int32, shape, 0) // row_size
        col = lax.broadcasted_iota(jnp.int32, shape, 1) // col_size
        return jnp.where(row == col, 1.0, 0.0).astype(jnp.bfloat16)

    block = indicator((wide, wide), members, members)
    slot_block = indicator((wide, LANE), members, SLOTS)
    eye = jnp.where(
        lax.broadcasted_iota(jnp.int32, (members, wide), 0)
        == lax.broadcasted_iota(jnp.int32, (members, wide), 1) % members,
        1.0,
        0.0,
    )
    spare_rows = jnp.zeros((15, wide), jnp.float32)
    per = LANE // members
    first_half = lax.broadcasted_iota(jnp.int32, (members, LANE), 1) < members
    first_half16 = jnp.where(first_half, 1.0, 0.0).astype(jnp.bfloat16)
    base = pl.program_id(0) * (groups * GROUP)

    def stacked(parts, mask):
        return [jnp.concatenate([part] * GROUP, axis=0) * mask for part in parts]

    def one(g):
        averages, anomalies = [], []
        spread = jnp.zeros((members, LANE), jnp.float32)
        there = jnp.zeros((8, LANE), jnp.float32)
        row = pl.ds(row_of(g), 1)
        index = jnp.broadcast_to(obs_ref[0, row, :].astype(jnp.int32), (members, LANE))
        for b in range(GROUP):
            x = tile_of(x_ref, (0 if blocked else base) + g * GROUP + b)[...]
            average = jnp.mean(x, axis=0, keepdims=True)
            anomaly = x - average
            averages.append(average)
            anomalies.append(anomaly)
            seen = jnp.take_along_axis(anomaly, index, axis=1, mode="promise_in_bounds")
            spread = jnp.where(slots_of[b], seen, spread)
            mean_seen = jnp.take_along_axis(
                jnp.broadcast_to(average, (8, LANE)), index[:8], axis=1, mode="promise_in_bounds"
            )
            there = jnp.where(slots_of[b], mean_seen, there)
        root = obs_ref[1, row, :]
        scaled = spread * root
        innovation = root * (obs_ref[2, row, :] - there[:1])
        yield
        scaled_split = split(scaled)
        wanted = jnp.concatenate([innovation, spare_rows[:, :LANE]], axis=0)
        left = [jnp.concatenate(pair, axis=0) for pair in zip(scaled_split, split(wanted))]
        stage = product(left, stacked(scaled_split, slot_block), 1)
        system = stage[:members] + spare * eye
        wanted = stage[members:]
        yield
        squares = jnp.sum(system * system, axis=0, keepdims=True)
        pieces = split(squares, 3) + [jnp.zeros((13, wide), jnp.bfloat16)]
        total = jnp.sum(mm(jnp.concatenate(pieces, axis=0), block), axis=0, keepdims=True)
        yield
        inverse = 1.0 / jnp.sqrt(total)
        root_norm = jnp.sqrt(inverse)
        system = system * inverse
        result = None
        for number in range(SWEEPS):
            factor = 1.5 * eye - 0.5 * system
            right = stacked(split(factor), block)
            last = number == SWEEPS - 1
            if last:
                result = times(result, right)
            elif number == 0:
                stage, result = times(system, right), factor
            else:
                stage = times(jnp.concatenate([system, result], axis=0), right)
                result = stage[members:]
            yield
            if not last:
                system = times(stage[:members], right)
                yield
        right = stacked(split(result), block)
        wanted = times(wanted, right)
        yield
        mean_weight = times(wanted, right)[:1] * inverse
        yield
        high, low = split((spare**0.5 * root_norm) * result + mean_weight)
        for b in range(GROUP):
            at = LANE * (b // per)
            here, there_low = high[:, at : at + LANE], low[:, at : at + LANE]
            turned = lambda part: pltpu.roll(part.astype(jnp.float32), members, 1).astype(jnp.bfloat16)
            if b % per:
                left = jnp.where(first_half, turned(here), there_low)
            else:
                left = jnp.where(first_half, here, turned(there_low))
            left = jnp.concatenate([left, left * first_half16], axis=1)
            a_high, a_low = split(anomalies[b])
            right = jnp.concatenate([a_high, a_high, a_low, jnp.zeros_like(a_low)], axis=0)
            tile_of(out_ref, first + base + g * GROUP + b)[...] = mm(left, right) + averages[b]
        yield

    running = [one(g) for g in range(groups)]
    while running:
        running = [r for r in running if next(r, running) is None]


def analyse(background, observations, groups, total, first, row_of, earlier=None):
    members, rows, width = background.shape
    tiles = groups * GROUP
    kernel = functools.partial(analysis_kernel, groups=groups, first=first, row_of=row_of)
    call = functools.partial(
        pl.pallas_call,
        grid=(rows // tiles,),
        out_shape=pltpu.VMEM((members, total, width), jnp.float32),
        out_specs=vmem(),
        compiler_params=pltpu.CompilerParams(vmem_limit_bytes=32 << 20),
        name="analysis",
    )
    if earlier is None:
        field = pl.BlockSpec((members, tiles, width), lambda i: (0, i, 0))
        background = pltpu.with_memory_space_constraint(background, pltpu.HBM)
        return call(functools.partial(kernel, blocked=True), in_specs=[vmem(), field])(observations, background)
    return call(
        lambda o, x, _, out: kernel(o, x, out),
        in_specs=[vmem()] * 3,
        input_output_aliases={2: 0},
    )(observations, resident(background), resident(earlier))


def exchange(x, axes=MEMBER):
    return lax.all_to_all(x, axes, 0, 0, tiled=True)


def per_device(ensemble, velocity, observed_column, slot_count, radius, observed_value, error_variance):
    members, height, width = ensemble.shape
    ensemble, velocity = (pltpu.with_memory_space_constraint(a, pltpu.HBM) for a in (ensemble, velocity))
    devices = lax.axis_size("tile")
    here = lax.axis_index("tile")
    edge = height // 8
    kept = height - 2 * edge
    groups = 2 * edge // GROUP
    half = groups // 2
    inner_row = lambda g: half + groups * pl.program_id(0) + g
    outer_row = lambda g: g if g < half else height // GROUP - groups + g

    columns = observed_column[:, 0]
    values = observed_value[:, 0]
    active = (jnp.arange(SLOTS, dtype=jnp.int32)[None, :] < slot_count).astype(jnp.float32)
    offset = (columns.astype(jnp.float32) - 0.5 * (COLS - 1)) / radius.astype(jnp.float32)
    root_weight = jnp.sqrt(active / (1.0 + offset * offset) / error_variance[:, 0])
    observations = jnp.stack([columns.astype(jnp.float32), root_weight, values])
    observations = observations.reshape(3, height // GROUP, LANE)

    core = lax.axis_index(CORE)
    edges = jnp.stack([here == 0, here == devices - 1, here % 2 == 1, core == 1]).astype(jnp.int32)
    first, to_near, to_far = forecast_inner(edges, ensemble, velocity, edge, kept)
    near = lax.ppermute(to_near, "tile", [(i, i ^ 1) for i in range(devices)])
    first = exchange(first.reshape(-1, kept, COLS))
    inside = range(1, devices - 1)
    far = lax.ppermute(to_far, "tile", [(i, i + 1 if i % 2 else i - 1) for i in inside])
    second = forecast_edge(edges, ensemble, velocity, near, far, edge)
    swapped = lax.ppermute(second[1], CORE, [(0, 1), (1, 0)])
    second = merge(edges, second, swapped)
    second = exchange(second.reshape(-1, 2 * edge, COLS), CHIP)
    done = analyse(first, observations, groups, height, 0, inner_row)
    done = analyse(second, observations, groups, height, kept, outer_row, done)
    done = exchange(done)
    both = jnp.concatenate([done[:, kept : kept + edge], done[:, :kept], done[:, kept + edge :]], axis=1)
    both = both.reshape(-1, members, height, COLS)
    return both.transpose(1, 2, 0, 3).reshape(members, height, width)


def solution(mesh):
    torus = Mesh(mesh.devices.reshape(4, 4, 2, mesh.shape["tile"]), (*MEMBER, "tile"))
    return jax.shard_map(
        per_device,
        mesh=torus,
        in_specs=(
            P(MEMBER, "tile", None),
            P(None, "tile", None),
            P("tile", MEMBER, None),
            P("tile", MEMBER),
            P("tile", MEMBER),
            P("tile", MEMBER, None),
            P("tile", MEMBER, None),
        ),
        out_specs=P(MEMBER, "tile", None),
        check_vma=False,
    )
```
